256 devices in a mesh: grp: 4 (over y), tok: 16 (over z, core), head: 4 (over x).
Axes of the slice: x: 4, y: 4, z: 8, core: 2. Of those that a mesh axis runs over, the one named last changes fastest.
Arguments:
- tokens: bfloat16 [4, 2048, 1024], P('grp', 'tok'), may hold values from -6 to 6
- lengths: int32 [4, 8], P('grp'), may hold values from 1 to 1536, 2048 in all within a row
- block_position: int32 [4, 256], P('grp'), may hold values from 0 to 255, each once within a row
- prefix_pool: bfloat16 [4, 256, 16, 2, 1024], P('grp', ('tok', 'head'))
- cross_cache: bfloat16 [4, 256, 2, 1024], P('grp', None, None, 'head')
- w_query: bfloat16 [1024, 1024], P(None, 'head'), may hold values from -0.5 to 0.5
- w_keyvalue: bfloat16 [1024, 2, 1024], P(None, None, 'head'), may hold values from -0.1875 to 0.1875
- w_out: bfloat16 [1024, 1024], P('head'), may hold values from -0.1875 to 0.1875
- w_cross_query: bfloat16 [1024, 1024], P(None, 'head'), may hold values from -0.5 to 0.5
- w_cross_out: bfloat16 [1024, 1024], P('head'), may hold values from -0.1875 to 0.1875
- w_up: bfloat16 [1024, 8192], P(None, 'head'), may hold values from -0.1875 to 0.1875
- w_down: bfloat16 [8192, 1024], P('head'), may hold values from -0.0625 to 0.0625
Outputs:
- layer_out: bfloat16 [4, 2048, 1024], P('grp', ('tok', 'head'))
The draws below stay inside these ranges and needn't reach their ends.
Inputs may be any that keep to these rules, and one draw needn't show every extreme that they name: Each group's 8 lengths sum to 2048; the longest is exactly 1536. `block_position`: each group's row is a permutation of 0 to 255.
All inputs are finite; a program needn't handle non-finite values.
Results may differ from the reference program's by a relative error of at most 0.034.
The reference program's roundings to bfloat16 on the way count: a program that leaves them out, or rounds other values in their place, can miss the bound.
Values may be sent and summed in bfloat16 or wider, within the bound.
A program may use at most 128 MiB of HBM per device.

```python
import math
import jax
import jax.numpy as jnp
import numpy as np
from jax import lax

D = 1024
HEADS = 16
HEAD_DIM = 64
FF = 8192
TOK_DEV = 128
E = 256
BLK = 16
SINK = 4
REQS = 8
GROUPS = 4
SUFFIX = 2048
NBLOCKS = 256
PREFIX = 4096
WINDOW = 1024


def boosted_cache(key, lead_shape, value_scale):
    normal_draw = jax.random.truncated_normal(jax.random.fold_in(key, 11), -6.0, 6.0, lead_shape + (2, D), jnp.float32)
    half_scale = jnp.where(jnp.arange(2)[:, None] == 0, 1.0, value_scale).astype(jnp.float32)
    normal_draw = normal_draw * half_scale
    return normal_draw


def draw_prefix_pool(key, part):
    return boosted_cache(key, (GROUPS, NBLOCKS, BLK), 3.0).astype(jnp.bfloat16)


def draw_cross_cache(key, part):
    return boosted_cache(key, (GROUPS, E), 1.0).astype(jnp.bfloat16)


def shard_levels(rng, extent, split, low, top_value):
    def one(position, parts):
        steps = jax.random.uniform(jax.random.fold_in(jax.random.fold_in(rng, 6), position), (parts,), jnp.float32, low / len(split), top_value / len(split))
        return jnp.repeat(jnp.exp(steps), extent[position] // parts).reshape((-1,) + (1,) * (len(extent) - position - 1))

    level = one(*split[0])
    for cut in split[1:]:
        level = level * one(*cut)
    return level


def profile(count, total, bound, lean):
    portions = [(1 << 20) // math.isqrt(rank ** lean) + 1 for rank in range(2, count + 1)]
    spare, given = total - bound - (count - 1), [1] * (count - 1)
    while spare > 0:
        free = [i for i in range(count - 1) if given[i] < bound]
        mass, remaining = sum([portions[i] for i in free]), spare
        for i in free:
            extra = min(bound - given[i], max(1, remaining * portions[i] // mass), spare)
            given[i] = given[i] + extra
            spare = spare - extra
    return np.array([bound] + given)


def ragged_sizes(stream_key, number_of, total, reach, lean):
    if number_of == 2:
        one = jax.random.randint(stream_key, (), max(1, total - reach), min(reach, total - 1) + 1)
        return jnp.stack([one, total - one])
    sizes = jnp.asarray(profile(number_of, total, reach, lean), jnp.int32)
    pairs = (number_of - 1) // 2
    giver, receiver = sizes[1:1 + 2 * pairs:2], sizes[2:2 + 2 * pairs:2]
    room = jnp.minimum(giver - 1, reach - receiver)
    shifted = jax.random.randint(jax.random.fold_in(stream_key, 1), (pairs,), 0, 1 << 20) % (room + 1)
    sizes = sizes.at[1:1 + 2 * pairs:2].set(giver - shifted).at[2:2 + 2 * pairs:2].set(receiver + shifted)
    return sizes[jax.random.permutation(jax.random.fold_in(stream_key, 2), number_of)]


def gaussian(rng, dims, width, bound, split=(), kind=jnp.bfloat16):
    drawn = width * jax.random.normal(rng, dims, jnp.float32)
    if split:
        drawn = drawn * shard_levels(rng, dims, split, -0.22, 0.18)
    return jnp.clip(drawn, -bound, bound).astype(kind)


def setup_inputs(seed: int = 0) -> dict:
    splits = jax.random.split(jax.random.key(seed), 13)
    return {
        "tokens": gaussian(splits[0], (GROUPS, SUFFIX, D), 1.0, 6.0, ((0, 4), (1, 16))),
        "lengths": jax.vmap(lambda own: ragged_sizes(own, REQS, SUFFIX, SUFFIX * 3 // 4, 2))(jax.random.split(splits[1], GROUPS)).reshape((GROUPS, REQS)).astype(jnp.int32),
        "block_position": jax.vmap(lambda own: jax.random.permutation(own, NBLOCKS))(jax.random.split(splits[2], GROUPS)).reshape((GROUPS, NBLOCKS)).astype(jnp.int32),
        "prefix_pool": draw_prefix_pool(jax.random.fold_in(splits[12], 71), 0),
        "cross_cache": draw_cross_cache(jax.random.fold_in(splits[12], 71), 0),
        "w_query": gaussian(splits[5], (D, D), (D // 8) ** -0.5, 0.5, ((1, 4),)),
        "w_keyvalue": gaussian(splits[6], (D, 2, D), D ** -0.5, 0.1875, ((2, 4),)),
        "w_out": gaussian(splits[7], (D, D), D ** -0.5, 0.1875, ((0, 4),)),
        "w_cross_query": gaussian(splits[8], (D, D), (D // 8) ** -0.5, 0.5, ((1, 4),)),
        "w_cross_out": gaussian(splits[9], (D, D), D ** -0.5, 0.1875, ((0, 4),)),
        "w_up": gaussian(splits[10], (D, FF), D ** -0.5, 0.1875, ((1, 4),)),
        "w_down": gaussian(splits[11], (FF, D), FF ** -0.5, 0.0625, ((0, 4),)),
    }


eps = 1e-05
masked = -1e+30

def layer_norm(values):
    center = values - lax.optimization_barrier(jnp.mean(values, axis=-1, keepdims=True))
    spread = lax.optimization_barrier(jnp.mean(center * center, axis=-1, keepdims=True))
    return center * lax.rsqrt(spread + eps)

def request_info(token_ids, lengths_row):
    request_ends = jnp.cumsum(lengths_row, dtype=jnp.int32)
    before = request_ends[None, :] <= token_ids[:, None]
    request = lax.optimization_barrier(jnp.sum(before.astype(jnp.int32), axis=1, dtype=jnp.int32))
    first_token = lax.optimization_barrier(jnp.sum(jnp.where(before, lengths_row[None, :], 0), axis=1, dtype=jnp.int32))
    return (request, token_ids - first_token)

def softmax_heads(queries, key_heads, value_heads, allowed, score_scale):
    scores = jnp.einsum('qhd,khd->hqk', queries.astype(jnp.float32), key_heads.astype(jnp.float32)) * score_scale
    scores = jnp.where(allowed[None], scores, masked)
    row_max = lax.optimization_barrier(jnp.max(scores, axis=-1))
    weights = jnp.where(allowed[None], jnp.exp(scores - row_max[..., None]), 0.0)
    row_sum = lax.optimization_barrier(jnp.sum(weights, axis=-1))
    summed = jnp.einsum('hqk,khd->hqd', weights.astype(jnp.bfloat16).astype(jnp.float32), value_heads.astype(jnp.float32))
    result = summed / row_sum[..., None]
    return jnp.transpose(result, (1, 0, 2)).reshape(queries.shape[0], -1).astype(jnp.bfloat16)

def reference(tokens, lengths, block_position, prefix_pool, cross_cache, w_query, w_keyvalue, w_out, w_cross_query, w_cross_out, w_up, w_down):
    score_scale = HEAD_DIM ** (-0.5)
    outputs = []
    for group_index in range(GROUPS):
        residual = tokens[group_index].astype(jnp.float32)
        normed = layer_norm(residual).astype(jnp.bfloat16)
        queries = jnp.dot(normed, w_query, preferred_element_type=jnp.float32).astype(jnp.bfloat16)
        keyvalue = jnp.dot(normed, w_keyvalue.reshape(D, 2 * D), preferred_element_type=jnp.float32).astype(jnp.bfloat16).reshape(SUFFIX, 2, D)
        lengths_row = lengths[group_index]
        all_ids = jnp.arange(SUFFIX, dtype=jnp.int32)
        request, offset = request_info(all_ids, lengths_row)
        padded = jnp.concatenate([jnp.zeros((WINDOW, 2, D), jnp.bfloat16), keyvalue], axis=0)
        block_table = block_position[group_index]
        places = (block_table[:, None] * BLK + jnp.arange(BLK, dtype=jnp.int32)[None, :]).reshape(-1)
        pool = prefix_pool[group_index].reshape(PREFIX, 2, D)

        def one_block(block_index):
            first_row = (block_index * TOK_DEV).astype(jnp.int32)
            own_ids = first_row + jnp.arange(TOK_DEV, dtype=jnp.int32)
            own_request = lax.dynamic_slice_in_dim(request, first_row, TOK_DEV, 0)
            own_offset = lax.dynamic_slice_in_dim(offset, first_row, TOK_DEV, 0)
            block_queries = lax.dynamic_slice_in_dim(queries, first_row, TOK_DEV, 0).reshape(TOK_DEV, HEADS, HEAD_DIM)
            near_keys = lax.dynamic_slice_in_dim(padded, first_row, WINDOW + TOK_DEV, 0)
            near_ids = first_row - WINDOW + jnp.arange(WINDOW + TOK_DEV, dtype=jnp.int32)
            near_request = request_info(near_ids, lengths_row)[0]
            near_allowed = (near_ids[None, :] >= 0) & (near_request[None, :] == own_request[:, None]) & (near_ids[None, :] <= own_ids[:, None]) & (own_ids[:, None] - near_ids[None, :] < WINDOW)
            prefix_allowed = (places[None, :] < SINK) | (places[None, :] > PREFIX + own_offset[:, None] - WINDOW)
            all_keys = jnp.concatenate([near_keys, pool], axis=0)
            allowed = jnp.concatenate([near_allowed, prefix_allowed], axis=1)
            key_heads = all_keys[:, 0].reshape(-1, HEADS, HEAD_DIM)
            value_heads = all_keys[:, 1].reshape(-1, HEADS, HEAD_DIM)
            return softmax_heads(block_queries, key_heads, value_heads, allowed, score_scale)
        attended = lax.map(one_block, jnp.arange(SUFFIX // TOK_DEV, dtype=jnp.int32)).reshape(SUFFIX, D)
        after_self = residual + jnp.dot(attended, w_out, preferred_element_type=jnp.float32)
        cross_query = jnp.dot(layer_norm(after_self).astype(jnp.bfloat16), w_cross_query, preferred_element_type=jnp.float32).astype(jnp.bfloat16)
        cross_keys = cross_cache[group_index][:, 0].reshape(E, HEADS, HEAD_DIM)
        cross_values = cross_cache[group_index][:, 1].reshape(E, HEADS, HEAD_DIM)
        cross_allowed = jnp.ones((SUFFIX, E), dtype=bool)
        cross_out = softmax_heads(cross_query.reshape(SUFFIX, HEADS, HEAD_DIM), cross_keys, cross_values, cross_allowed, score_scale)
        after_cross = after_self + jnp.dot(cross_out, w_cross_out, preferred_element_type=jnp.float32)
        hidden = jax.nn.relu(jnp.dot(layer_norm(after_cross).astype(jnp.bfloat16), w_up, preferred_element_type=jnp.float32)).astype(jnp.bfloat16)
        result = after_cross + jnp.dot(hidden, w_down, preferred_element_type=jnp.float32)
        outputs.append(result.astype(jnp.bfloat16))
    return jnp.stack(outputs, axis=0)
```

```python
import functools

import jax
import jax.numpy as jnp
from jax import lax
from jax.experimental import pallas as pl
from jax.experimental.pallas import tpu as pltpu
from jax.sharding import PartitionSpec as P

HEAD_DIM = 64
SINK = 4
WINDOW = 1024
EPS = 1e-05
MASKED = -1e30
MESH = pl.DeviceIdType.MESH

ROWS = 128
WIDTH = 1024
COLS = 256
SHARE = 32
BLK = 16
NZ = 8
SFX_HOPS = 4
F32 = jnp.float32
BF16 = jnp.bfloat16


def layer_norm(v):
    center = v - jnp.mean(v, axis=-1, keepdims=True)
    spread = jnp.mean(center * center, axis=-1, keepdims=True)
    return center * lax.rsqrt(spread + EPS)


def dot(a, b):
    return jnp.dot(a, b, preferred_element_type=F32)


def dot_t(a, b):
    return lax.dot_general(a, b, (((1,), (1,)), ((), ())), preferred_element_type=F32)


def stack_heads(q):
    head = lax.broadcasted_iota(jnp.int32, q.shape, 1) // HEAD_DIM
    zero = jnp.zeros_like(q)
    return jnp.concatenate([jnp.where(head == i, q, zero) for i in range(4)], axis=0)


def unstack_heads(summed, total, rows):
    head = lax.broadcasted_iota(jnp.int32, (rows, COLS), 1) // HEAD_DIM
    num = summed[0:rows]
    den = jnp.broadcast_to(total[0:rows], (rows, COLS))
    for i in range(1, 4):
        part = slice(i * rows, (i + 1) * rows)
        num = jnp.where(head == i, summed[part], num)
        den = jnp.where(head == i, jnp.broadcast_to(total[part], (rows, COLS)), den)
    return (num / den).astype(BF16)


def layer_kernel(
    cap,
    plus_hops,
    lengths_ref,
    tokens_ref,
    pool_ref,
    target_ref,
    places_ref,
    cross_ref,
    wq_hbm,
    wkv_hbm,
    wout_hbm,
    wcq_hbm,
    wco_hbm,
    wup_hbm,
    wdown_hbm,
    out_ref,
    wq,
    wkv,
    wout,
    wcq,
    wco,
    wup,
    wdown,
    raw,
    sfx,
    pk,
    qbd,
    scores,
    rs_send,
    rs_recv,
    ag,
    w_sem,
    local_sem,
    x_send,
    x_recv,
    sib_send,
    sib_recv,
    sfx_send,
    sfx_recv,
    sfx_sib_send,
    sfx_sib_recv,
    plus_send,
    plus_recv,
    minus_send,
    minus_recv,
    pk_sib_send,
    pk_sib_recv,
    rs_s,
    rs_r,
    ag_s,
    ag_r,
):
    minus_hops = NZ - 1 - plus_hops
    lane = cap * BLK
    t = lax.axis_index("tok")
    h = lax.axis_index("head")
    core = lax.rem(t, 2)
    z = t // 2
    sib = t + 1 - 2 * core
    up = lax.rem(t + 2, 2 * NZ)
    down = lax.rem(t + 2 * NZ - 2, 2 * NZ)

    def peer(r):
        return lax.rem(h + r, 4)

    loads = [
        pltpu.make_async_copy(src, dst, w_sem.at[i])
        for i, (src, dst) in enumerate(
            [
                (wq_hbm, wq),
                (wkv_hbm, wkv),
                (wout_hbm, wout),
                (wcq_hbm, wcq),
                (wco_hbm, wco),
                (wup_hbm, wup),
                (wdown_hbm, wdown),
            ]
        )
    ]
    for c in loads:
        c.start()

    barrier = pltpu.get_barrier_semaphore()
    for dev in ({"head": peer(1)}, {"head": peer(2)}, {"head": peer(3)}, {"tok": sib}, {"tok": up}, {"tok": down}):
        pl.semaphore_signal(barrier, inc=1, device_id=dev, device_id_type=MESH)
    pl.semaphore_wait(barrier, 6)

    def remote(src, dst, send, recv, dev):
        return pltpu.make_async_remote_copy(
            src_ref=src, dst_ref=dst, send_sem=send, recv_sem=recv, device_id=dev, device_id_type=MESH
        )

    sent = []

    def go(c):
        c.start()
        sent.append(c)
        return c

    raw_rows = raw.at[pl.ds(pl.multiple_of(core * 256, 256) + pl.multiple_of(h * 64, 64), 64)]
    x_copies = [
        go(remote(pool_ref.at[peer(r)], raw_rows, x_send.at[r], x_recv.at[r], {"head": peer(r)}))
        for r in (1, 2, 3)
    ]
    own_copy = pltpu.make_async_copy(pool_ref.at[h], raw_rows, local_sem.at[0])
    own_copy.start()

    normed = layer_norm(tokens_ref[...].astype(F32)).astype(BF16)
    loads[1].wait()
    sfx[0, pl.ds(pl.multiple_of(core * ROWS, ROWS), ROWS), :] = dot(normed, wkv[...]).astype(BF16)
    my_rows = pl.ds(pl.multiple_of(core * ROWS, ROWS), ROWS)
    my_lane = pl.ds(pl.multiple_of(core * lane, lane), lane)

    def sfx_hop(d):
        return remote(
            sfx.at[d, my_rows], sfx.at[d + 1, my_rows], sfx_send.at[d + 1], sfx_recv.at[d + 1], {"tok": up}
        )

    def sfx_side(d):
        return remote(
            sfx.at[d, my_rows], sfx.at[d, my_rows], sfx_sib_send.at[d], sfx_sib_recv.at[d], {"tok": sib}
        )

    def plus_hop(d):
        return remote(pk.at[d, my_lane], pk.at[d + 1, my_lane], plus_send.at[d + 1], plus_recv.at[d + 1], {"tok": up})

    def minus_hop(d):
        src = (NZ - d) % NZ
        return remote(
            pk.at[src, my_lane], pk.at[NZ - d - 1, my_lane], minus_send.at[d + 1], minus_recv.at[d + 1], {"tok": down}
        )

    def pk_side(d):
        return remote(pk.at[d, my_lane], pk.at[d, my_lane], pk_sib_send.at[d], pk_sib_recv.at[d], {"tok": sib})

    sfx_copies = {1: go(sfx_hop(0))}
    sfx_sides = {0: go(sfx_side(0))}

    loads[0].wait()
    q = (dot(normed, wq[...]) * (HEAD_DIM ** -0.5)).astype(BF16)
    qbd[...] = stack_heads(q)

    own_copy.wait()
    for c in x_copies:
        c.wait_recv()
    half = pl.ds(pl.multiple_of(core * 256, 256), 256)
    raw_side = go(remote(raw.at[half], raw.at[half], sib_send.at[0], sib_recv.at[0], {"tok": sib}))
    raw_side.wait_recv()
    slot = lax.broadcasted_iota(jnp.int32, (lane, 512), 0) + core * lane
    pick = (target_ref[pl.ds(z, 1), :] == slot).astype(F32).astype(BF16)
    pk[0, my_lane, :] = dot(pick, raw[...]).astype(BF16)
    plus_copies = {1: go(plus_hop(0))}
    minus_copies = {1: go(minus_hop(0))}
    pk_sides = {0: go(pk_side(0))}

    own_id = t * ROWS + lax.broadcasted_iota(jnp.int32, (ROWS, 256), 0)
    first = jnp.zeros((ROWS, 256), jnp.int32)
    end = jnp.int32(0)
    for i in range(8):
        length = lengths_ref[0, i]
        end = end + length
        first = first + jnp.where(own_id >= end, length, 0)
    low = jnp.maximum(first, own_id - (WINDOW - 1))
    beyond = NZ * 32 * BLK - WINDOW + own_id - first
    col = lax.broadcasted_iota(jnp.int32, (ROWS, 256), 1)

    tops = [jnp.full((4 * ROWS, 128), MASKED, F32)]
    offset_of = {}

    def score(keys, allowed, offset):
        n = keys.shape[0]
        s = dot_t(qbd[...], keys)
        s = jnp.where(allowed[None], s.reshape(4, ROWS, n), MASKED).reshape(4 * ROWS, n)
        scores[:, offset : offset + n] = s
        top = tops[0]
        for j in range(n // 128):
            top = jnp.maximum(top, s[:, j * 128 : (j + 1) * 128])
        tops[0] = top

    def score_sfx(d):
        ids = (z - d) * 256 + col
        allowed = (ids >= low) & (ids <= own_id)
        score(sfx[d, :, 0:COLS], allowed, d * 256)

    base = (SFX_HOPS + 1) * 256

    def score_pk(d):
        row = lax.rem(z - d + NZ, NZ)
        for j in range(2 * lane // 256):
            place = places_ref[pl.ds(row, 1), j * 256 : (j + 1) * 256]
            place = jnp.broadcast_to(place, (ROWS, 256))
            allowed = ((place >= 0) & (place < SINK)) | (place > beyond)
            score(pk[d, j * 256 : (j + 1) * 256, 0:COLS], allowed, base + d * 2 * lane + j * 256)

    ready_sfx, ready_pk = [0], [0]
    for step in range(1, max(SFX_HOPS, plus_hops, minus_hops) + 2):
        next_sfx, next_pk = [], []
        if step <= SFX_HOPS:
            sfx_copies[step].wait_recv()
            if step < SFX_HOPS:
                sfx_copies[step + 1] = go(sfx_hop(step))
            sfx_sides[step] = go(sfx_side(step))
            next_sfx.append(step)
        if step <= minus_hops:
            minus_copies[step].wait_recv()
            if step < minus_hops:
                minus_copies[step + 1] = go(minus_hop(step))
            pk_sides[NZ - step] = go(pk_side(NZ - step))
            next_pk.append(NZ - step)
        if step <= plus_hops:
            plus_copies[step].wait_recv()
            if step < plus_hops:
                plus_copies[step + 1] = go(plus_hop(step))
            pk_sides[step] = go(pk_side(step))
            next_pk.append(step)
        for d in ready_sfx:
            sfx_sides[d].wait_recv()
            score_sfx(d)
        for d in ready_pk:
            pk_sides[d].wait_recv()
            score_pk(d)
        ready_sfx, ready_pk = next_sfx, next_pk

    top = jnp.max(tops[0], axis=-1, keepdims=True)
    summed = jnp.zeros((4 * ROWS, COLS), F32)
    totals = jnp.zeros((4 * ROWS, 128), F32)
    chunks = [(d * 256, sfx, d, 0) for d in range(SFX_HOPS + 1)] + [
        (base + d * 2 * lane + j * 256, pk, d, j) for d in range(NZ) for j in range(2 * lane // 256)
    ]
    for offset, buf, d, j in chunks:
        w = jnp.exp(scores[:, offset : offset + 256] - top)
        totals = totals + w[:, 0:128] + w[:, 128:256]
        summed = summed + dot(w.astype(BF16), buf[d, j * 256 : (j + 1) * 256, COLS : 2 * COLS])
    attended = unstack_heads(summed, jnp.sum(totals, axis=-1, keepdims=True), ROWS)

    my_share = pl.ds(pl.multiple_of(h * SHARE, SHARE), SHARE)

    def reduce_scatter(i, partial):
        rs_send[i] = partial.astype(BF16)
        copies = [
            go(
                remote(
                    rs_send.at[i, pl.ds(pl.multiple_of(peer(r) * SHARE, SHARE), SHARE)],
                    rs_recv.at[i, r],
                    rs_s.at[i, r],
                    rs_r.at[i, r],
                    {"head": peer(r)},
                )
            )
            for r in (2, 1, 3)
        ]
        total = rs_send[i, my_share, :].astype(F32)
        for c in copies:
            c.wait_recv()
        for r in (1, 2, 3):
            total = total + rs_recv[i, r].astype(F32)
        return total

    def all_gather(i, rows):
        ag[i, my_share, :] = rows
        copies = [
            go(
                remote(
                    ag.at[i, my_share], ag.at[i, my_share], ag_s.at[i, r], ag_r.at[i, r], {"head": peer(r)}
                )
            )
            for r in (2, 1, 3)
        ]
        for c in copies:
            c.wait_recv()
        return ag[i]

    loads[2].wait()
    after_self = tokens_ref[my_share, :].astype(F32) + reduce_scatter(0, dot(attended, wout[...]))
    x = all_gather(0, layer_norm(after_self).astype(BF16))
    loads[3].wait()
    cq = (dot(x, wcq[...]) * (HEAD_DIM ** -0.5)).astype(BF16)
    s = dot_t(stack_heads(cq), cross_ref[:, 0:COLS])
    w = jnp.exp(s - jnp.max(s, axis=-1, keepdims=True))
    cross_out = unstack_heads(
        dot(w.astype(BF16), cross_ref[:, COLS : 2 * COLS]), jnp.sum(w, axis=-1, keepdims=True), ROWS
    )
    loads[4].wait()
    after_cross = after_self + reduce_scatter(1, dot(cross_out, wco[...]))
    x = all_gather(1, layer_norm(after_cross).astype(BF16))
    loads[5].wait()
    hidden = jnp.maximum(dot(x, wup[...]), 0.0).astype(BF16)
    loads[6].wait()
    out_ref[...] = (after_cross + reduce_scatter(2, dot(hidden, wdown[...]))).astype(BF16)

    for c in sent:
        c.wait_send()


def run_layer(cap, plus_hops, lengths, tokens, pool, target, places, cross, *weights):
    lane = cap * BLK
    minus_hops = NZ - 1 - plus_hops
    keys = (SFX_HOPS + 1) * 256 + NZ * 2 * lane
    dma = pltpu.SemaphoreType.DMA
    vmem = pl.BlockSpec(memory_space=pltpu.VMEM)
    return pl.pallas_call(
        functools.partial(layer_kernel, cap, plus_hops),
        out_shape=jax.ShapeDtypeStruct((SHARE, WIDTH), BF16),
        in_specs=[pl.BlockSpec(memory_space=pltpu.SMEM)]
        + [vmem] * 5
        + [pl.BlockSpec(memory_space=pl.ANY)] * len(weights),
        out_specs=vmem,
        scratch_shapes=[pltpu.VMEM(w.shape, BF16) for w in weights]
        + [
            pltpu.VMEM((512, 2 * COLS), BF16),
            pltpu.VMEM((SFX_HOPS + 1, 256, 2 * COLS), BF16),
            pltpu.VMEM((NZ, 2 * lane, 2 * COLS), BF16),
            pltpu.VMEM((4 * ROWS, COLS), BF16),
            pltpu.VMEM((4 * ROWS, keys), F32),
            pltpu.VMEM((3, ROWS, WIDTH), BF16),
            pltpu.VMEM((3, 4, SHARE, WIDTH), BF16),
            pltpu.VMEM((2, ROWS, WIDTH), BF16),
            dma((len(weights),)),
            dma((1,)),
            dma((4,)),
            dma((4,)),
            dma((1,)),
            dma((1,)),
            dma((SFX_HOPS + 1,)),
            dma((SFX_HOPS + 1,)),
            dma((SFX_HOPS + 1,)),
            dma((SFX_HOPS + 1,)),
            dma((plus_hops + 1,)),
            dma((plus_hops + 1,)),
            dma((minus_hops + 1,)),
            dma((minus_hops + 1,)),
            dma((NZ,)),
            dma((NZ,)),
            dma((3, 4)),
            dma((3, 4)),
            dma((2, 4)),
            dma((2, 4)),
        ],
        compiler_params=pltpu.CompilerParams(
            collective_id=0, has_side_effects=True, vmem_limit_bytes=56 << 20
        ),
    )(lengths, tokens, pool, target, places, cross, *weights)


def on_device(
    tokens,
    lengths,
    block_position,
    prefix_pool,
    cross_cache,
    w_query,
    w_keyvalue,
    w_out,
    w_cross_query,
    w_cross_out,
    w_up,
    w_down,
):
    cap = 16
    pool = prefix_pool.reshape(64, 2, 4, COLS).transpose(2, 0, 1, 3).reshape(4, 64, 2 * COLS)
    table = block_position.reshape(NZ, 32)
    needed = (table == 0) | (table >= 192)
    index = jnp.arange(32, dtype=jnp.int32)
    rank = jnp.sum(
        jnp.where((index[None, :] < index[:, None])[None], needed[:, None, :], False).astype(jnp.int32), axis=2
    )
    rank = jnp.where(needed, rank, -1)
    inner = jnp.arange(BLK, dtype=jnp.int32)
    target = jnp.where(rank[:, :, None] < 0, -1, rank[:, :, None] * BLK + inner).reshape(NZ, 32 * BLK)
    slots = jnp.arange(2 * cap, dtype=jnp.int32)
    held = rank[:, None, :] == slots[None, :, None]
    block = jnp.sum(jnp.where(held, table[:, None, :] + 1, 0), axis=2) - 1
    places = jnp.where(block[:, :, None] < 0, -1, block[:, :, None] * BLK + inner).reshape(NZ, 2 * cap * BLK)
    out = run_layer(
        cap,
        3,
        lengths,
        tokens[0],
        pool,
        target,
        places,
        cross_cache[0].reshape(-1, 2 * COLS),
        w_query,
        w_keyvalue.reshape(WIDTH, 2 * COLS),
        w_out,
        w_cross_query,
        w_cross_out,
        w_up,
        w_down,
    )
    return out[None]


def solution(mesh):
    return jax.shard_map(
        on_device,
        mesh=mesh,
        in_specs=(
            P("grp", "tok", None),
            P("grp", None),
            P("grp", None),
            P("grp", ("tok", "head"), None, None, None),
            P("grp", None, None, "head"),
            P(None, "head"),
            P(None, None, "head"),
            P("head", None),
            P(None, "head"),
            P("head", None),
            P(None, "head"),
            P("head", None),
        ),
        out_specs=P("grp", ("tok", "head"), None),
        check_vma=False,
    )
```

```python
import functools

import jax
import jax.numpy as jnp
from jax import lax
from jax.experimental import pallas as pl
from jax.experimental.pallas import tpu as pltpu
from jax.sharding import PartitionSpec as P

HEAD_DIM = 64
SINK = 4
WINDOW = 1024
EPS = 1e-05
MASKED = -1e30
MESH = pl.DeviceIdType.MESH

ROWS = 128
WIDTH = 1024
COLS = 256
SHARE = 32
BLK = 16
NZ = 8
SFX_HOPS = 4
F32 = jnp.float32
BF16 = jnp.bfloat16


def layer_norm(v):
    center = v - jnp.mean(v, axis=-1, keepdims=True)
    spread = jnp.mean(center * center, axis=-1, keepdims=True)
    return center * lax.rsqrt(spread + EPS)


def dot(a, b):
    return jnp.dot(a, b, preferred_element_type=F32)


def dot_t(a, b):
    return lax.dot_general(a, b, (((1,), (1,)), ((), ())), preferred_element_type=F32)


def stack_heads(q):
    head = lax.broadcasted_iota(jnp.int32, q.shape, 1) // HEAD_DIM
    zero = jnp.zeros_like(q)
    return jnp.concatenate([jnp.where(head == i, q, zero) for i in range(4)], axis=0)


def unstack_heads(summed, total, rows):
    head = lax.broadcasted_iota(jnp.int32, (rows, COLS), 1) // HEAD_DIM
    num = summed[0:rows]
    den = jnp.broadcast_to(total[0:rows], (rows, COLS))
    for i in range(1, 4):
        part = slice(i * rows, (i + 1) * rows)
        num = jnp.where(head == i, summed[part], num)
        den = jnp.where(head == i, jnp.broadcast_to(total[part], (rows, COLS)), den)
    return (num / den).astype(BF16)


def layer_kernel(
    cap,
    plus_hops,
    lengths_ref,
    table_ref,
    tokens_hbm,
    pool_hbm,
    cross_hbm,
    wq_hbm,
    wkv_hbm,
    wout_hbm,
    wcq_hbm,
    wco_hbm,
    wup_hbm,
    wdown_hbm,
    out_ref,
    flag_ref,
    tokens_ref,
    cross,
    wq,
    wkv,
    wout,
    wcq,
    wco,
    wup,
    wdown,
    raw,
    sfx,
    pk,
    places_ref,
    qbd,
    scores,
    rs_send,
    rs_recv,
    ag,
    flags,
    w_sem,
    local_sem,
    x_send,
    x_recv,
    y_send,
    y_recv,
    sib_send,
    sib_recv,
    sfx_send,
    sfx_recv,
    sfx_sib_send,
    sfx_sib_recv,
    plus_send,
    plus_recv,
    minus_send,
    minus_recv,
    pk_sib_send,
    pk_sib_recv,
    rs_s,
    rs_r,
    ag_s,
    ag_r,
):
    minus_hops = NZ - 1 - plus_hops
    lane = cap * BLK
    g = lax.axis_index("grp")
    t = lax.axis_index("tok")
    h = lax.axis_index("head")
    core = lax.rem(t, 2)
    z = t // 2
    sib = t + 1 - 2 * core
    up = lax.rem(t + 2, 2 * NZ)
    down = lax.rem(t + 2 * NZ - 2, 2 * NZ)

    def peer(r):
        return lax.rem(h + r, 4)

    def group(r):
        return lax.rem(g + r, 4)

    loads = [
        pltpu.make_async_copy(src, dst, w_sem.at[i])
        for i, (src, dst) in enumerate(
            [
                (tokens_hbm, tokens_ref),
                (wkv_hbm.reshape(2 * WIDTH, COLS), wkv),
                (wq_hbm, wq),
                (wout_hbm, wout),
                (wcq_hbm, wcq),
                (cross_hbm.reshape(512, COLS), cross),
                (wco_hbm, wco),
                (wup_hbm, wup),
                (wdown_hbm, wdown),
            ]
        )
    ]
    for c in loads[:3]:
        c.start()

    barrier = pltpu.get_barrier_semaphore()
    for dev in (
        [{"head": peer(r)} for r in (1, 2, 3)] + [{"grp": group(r)} for r in (1, 2, 3)] + [{"tok": i} for i in (sib, up, down)]
    ):
        pl.semaphore_signal(barrier, inc=1, device_id=dev, device_id_type=MESH)
    pl.semaphore_wait(barrier, 9)

    def remote(src, dst, send, recv, dev):
        return pltpu.make_async_remote_copy(
            src_ref=src, dst_ref=dst, send_sem=send, recv_sem=recv, device_id=dev, device_id_type=MESH
        )

    sent = []

    def go(c):
        c.start()
        sent.append(c)
        return c

    raw_rows = raw.at[pl.ds(pl.multiple_of(core * 512, 512) + pl.multiple_of(h * 128, 128), 128)]

    def pool_part(i):
        return pool_hbm.reshape(128, WIDTH).at[:, pl.ds(pl.multiple_of(i * COLS, COLS), COLS)]

    x_copies = [
        go(remote(pool_part(peer(r)), raw_rows, x_send.at[r], x_recv.at[r], {"head": peer(r)})) for r in (2, 1, 3)
    ]
    own_copy = pltpu.make_async_copy(pool_part(h), raw_rows, local_sem.at[0])
    own_copy.start()
    for c in loads[3:]:
        c.start()

    loads[0].wait()
    normed = layer_norm(tokens_ref[...].astype(F32)).astype(BF16)
    spread_row = lax.broadcasted_iota(jnp.int32, (128, 512), 0)
    spread_col = lax.broadcasted_iota(jnp.int32, (128, 512), 1)
    spread_to = 2 * spread_row + jnp.where(spread_col >= 256, 257, 0)
    spread = (spread_to == spread_col).astype(F32).astype(BF16)
    blocks = [normed[:, i * 128 : (i + 1) * 128] for i in range(8)]
    wide = dot(jnp.concatenate(blocks, axis=0), spread).astype(BF16)
    halves = [
        jnp.concatenate([wide[i * 128 : (i + 1) * 128, c : c + 256] for i in range(8)], axis=1) for c in (0, 256)
    ]
    my_rows = pl.ds(pl.multiple_of(core * ROWS, ROWS), ROWS)
    my_lane = pl.ds(pl.multiple_of(core * lane, lane), lane)
    loads[1].wait()
    kv = dot(jnp.concatenate(halves, axis=0), wkv[...]).astype(BF16)
    sfx[0, my_rows, 0:COLS] = kv[:ROWS]
    sfx[0, my_rows, COLS : 2 * COLS] = kv[ROWS:]

    def sfx_hop(d):
        return remote(
            sfx.at[d, my_rows], sfx.at[d + 1, my_rows], sfx_send.at[d + 1], sfx_recv.at[d + 1], {"tok": up}
        )

    def sfx_side(d):
        return remote(
            sfx.at[d, my_rows], sfx.at[d, my_rows], sfx_sib_send.at[d], sfx_sib_recv.at[d], {"tok": sib}
        )

    def plus_hop(d):
        return remote(pk.at[d, my_lane], pk.at[d + 1, my_lane], plus_send.at[d + 1], plus_recv.at[d + 1], {"tok": up})

    def minus_hop(d):
        src = (NZ - d) % NZ
        return remote(
            pk.at[src, my_lane], pk.at[NZ - d - 1, my_lane], minus_send.at[d + 1], minus_recv.at[d + 1], {"tok": down}
        )

    def pk_side(d):
        return remote(pk.at[d, my_lane], pk.at[d, my_lane], pk_sib_send.at[d], pk_sib_recv.at[d], {"tok": sib})

    sfx_copies = {1: go(sfx_hop(0))}
    sfx_sides = {0: go(sfx_side(0))}

    loads[2].wait()
    q = (dot(normed, wq[...]) * (HEAD_DIM ** -0.5)).astype(BF16)
    qbd[...] = stack_heads(q)

    table = jnp.broadcast_to(table_ref[...], (8, 256))
    needed = ((table == 0) | (table >= 192)).astype(F32)
    i0 = lax.broadcasted_iota(jnp.int32, (256, 256), 0)
    i1 = lax.broadcasted_iota(jnp.int32, (256, 256), 1)
    upto = ((i1 <= i0) & (i1 // 32 == i0 // 32)).astype(F32).astype(BF16)
    rank = dot_t(needed.astype(BF16), upto) * needed
    rank_col = dot_t(upto, needed.astype(BF16))[:, 0:1]
    flags[0] = (rank > 2 * cap).astype(jnp.int32)
    y_copies = [
        go(remote(flags.at[0], flags.at[r], y_send.at[r], y_recv.at[r], {"grp": group(r)})) for r in (1, 2, 3)
    ]
    slot_block = lax.broadcasted_iota(jnp.int32, (256, 2 * lane), 1) // BLK + 1
    held = (rank_col == slot_block.astype(F32)).astype(F32).astype(BF16)
    chip = lax.broadcasted_iota(jnp.int32, (8, 256), 1) // 32 == lax.broadcasted_iota(jnp.int32, (8, 256), 0)
    numbers = jnp.where(chip, (table + 1).astype(F32) * needed, 0.0).astype(BF16)
    places = (dot(numbers, held).astype(jnp.int32) - 1) * BLK
    places_ref[...] = places + lax.rem(lax.broadcasted_iota(jnp.int32, (8, 2 * lane), 1), BLK)
    e0 = lax.broadcasted_iota(jnp.int32, (256, 1024), 0)
    e1 = lax.broadcasted_iota(jnp.int32, (256, 1024), 1)
    enlarge = (e1 // 32 + z * 32 == e0).astype(F32).astype(BF16)
    target = (dot(rank.astype(BF16), enlarge)[0:1].astype(jnp.int32) - 1) * (2 * BLK)
    target = target + lax.rem(lax.broadcasted_iota(jnp.int32, (1, 1024), 1), 2 * BLK)
    slot = lax.broadcasted_iota(jnp.int32, (2 * lane, 1024), 0)
    slot = jnp.where(slot >= lane, 2 * (slot - lane) + 1, 2 * slot) + core * (2 * lane)
    pick = (target == slot).astype(F32).astype(BF16)

    own_copy.wait()
    for c in x_copies:
        c.wait_recv()
    half = pl.ds(pl.multiple_of(core * 512, 512), 512)
    raw_side = go(remote(raw.at[half], raw.at[half], sib_send.at[0], sib_recv.at[0], {"tok": sib}))
    raw_side.wait_recv()
    packed = dot(pick, raw[...]).astype(BF16)
    pk[0, my_lane, 0:COLS] = packed[:lane]
    pk[0, my_lane, COLS : 2 * COLS] = packed[lane:]
    plus_copies = {1: go(plus_hop(0))}
    minus_copies = {1: go(minus_hop(0))}
    pk_sides = {0: go(pk_side(0))}

    own_id = t * ROWS + lax.broadcasted_iota(jnp.int32, (ROWS, 256), 0)
    first = jnp.zeros((ROWS, 256), jnp.int32)
    end = jnp.int32(0)
    for i in range(8):
        length = lengths_ref[0, i]
        end = end + length
        first = first + jnp.where(own_id >= end, length, 0)
    low = jnp.maximum(first, own_id - (WINDOW - 1))
    beyond = NZ * 32 * BLK - WINDOW + own_id - first
    col = lax.broadcasted_iota(jnp.int32, (ROWS, 256), 1)

    tops = [jnp.full((4 * ROWS, 128), MASKED, F32)]
    offset_of = {}

    def score(keys, allowed, offset):
        n = keys.shape[0]
        s = dot_t(qbd[...], keys)
        s = jnp.where(allowed[None], s.reshape(4, ROWS, n), MASKED).reshape(4 * ROWS, n)
        scores[:, offset : offset + n] = s
        top = tops[0]
        for j in range(n // 128):
            top = jnp.maximum(top, s[:, j * 128 : (j + 1) * 128])
        tops[0] = top

    def score_sfx(d):
        ids = (z - d) * 256 + col
        allowed = (ids >= low) & (ids <= own_id)
        score(sfx[d, :, 0:COLS], allowed, d * 256)

    base = (SFX_HOPS + 1) * 256

    def score_pk(d):
        row = lax.rem(z - d + NZ, NZ)
        for j in range(2 * lane // 256):
            place = places_ref[pl.ds(row, 1), j * 256 : (j + 1) * 256]
            place = jnp.broadcast_to(place, (ROWS, 256))
            allowed = ((place >= 0) & (place < SINK)) | (place > beyond)
            score(pk[d, j * 256 : (j + 1) * 256, 0:COLS], allowed, base + d * 2 * lane + j * 256)

    ready_sfx, ready_pk = [0], [0]
    for step in range(1, max(SFX_HOPS, plus_hops, minus_hops) + 2):
        next_sfx, next_pk = [], []
        if step <= SFX_HOPS:
            sfx_copies[step].wait_recv()
            if step < SFX_HOPS:
                sfx_copies[step + 1] = go(sfx_hop(step))
            sfx_sides[step] = go(sfx_side(step))
            next_sfx.append(step)
        if step <= minus_hops:
            minus_copies[step].wait_recv()
            if step < minus_hops:
                minus_copies[step + 1] = go(minus_hop(step))
            pk_sides[NZ - step] = go(pk_side(NZ - step))
            next_pk.append(NZ - step)
        if step <= plus_hops:
            plus_copies[step].wait_recv()
            if step < plus_hops:
                plus_copies[step + 1] = go(plus_hop(step))
            pk_sides[step] = go(pk_side(step))
            next_pk.append(step)
        for d in ready_sfx:
            sfx_sides[d].wait_recv()
            score_sfx(d)
        for d in ready_pk:
            pk_sides[d].wait_recv()
            score_pk(d)
        ready_sfx, ready_pk = next_sfx, next_pk

    top = jnp.max(tops[0], axis=-1, keepdims=True)
    summed = jnp.zeros((4 * ROWS, COLS), F32)
    totals = jnp.zeros((4 * ROWS, 128), F32)
    chunks = [(d * 256, sfx, d, 0) for d in range(SFX_HOPS + 1)] + [
        (base + d * 2 * lane + j * 256, pk, d, j) for d in range(NZ) for j in range(2 * lane // 256)
    ]
    for offset, buf, d, j in chunks:
        w = jnp.exp(scores[:, offset : offset + 256] - top)
        totals = totals + w[:, 0:128] + w[:, 128:256]
        summed = summed + dot(w.astype(BF16), buf[d, j * 256 : (j + 1) * 256, COLS : 2 * COLS])
    attended = unstack_heads(summed, jnp.sum(totals, axis=-1, keepdims=True), ROWS)

    my_share = pl.ds(pl.multiple_of(h * SHARE, SHARE), SHARE)

    def reduce_scatter(i, partial):
        rs_send[i] = partial.astype(BF16)
        copies = [
            go(
                remote(
                    rs_send.at[i, pl.ds(pl.multiple_of(peer(r) * SHARE, SHARE), SHARE)],
                    rs_recv.at[i, r],
                    rs_s.at[i, r],
                    rs_r.at[i, r],
                    {"head": peer(r)},
                )
            )
            for r in (2, 1, 3)
        ]
        total = rs_send[i, my_share, :].astype(F32)
        for c in copies:
            c.wait_recv()
        for r in (1, 2, 3):
            total = total + rs_recv[i, r].astype(F32)
        return total

    def all_gather(i, rows):
        ag[i, my_share, :] = rows
        copies = [
            go(
                remote(
                    ag.at[i, my_share], ag.at[i, my_share], ag_s.at[i, r], ag_r.at[i, r], {"head": peer(r)}
                )
            )
            for r in (2, 1, 3)
        ]
        for c in copies:
            c.wait_recv()
        return ag[i]

    loads[3].wait()
    after_self = tokens_ref[my_share, :].astype(F32) + reduce_scatter(0, dot(attended, wout[...]))
    x = all_gather(0, layer_norm(after_self).astype(BF16))
    loads[4].wait()
    cq = (dot(x, wcq[...]) * (HEAD_DIM ** -0.5)).astype(BF16)
    loads[5].wait()
    s = dot_t(stack_heads(cq), cross[...])
    is_key = lax.rem(lax.broadcasted_iota(jnp.int32, (4 * ROWS, 512), 1), 2) == 0
    s = jnp.where(is_key, s, MASKED)
    w = jnp.exp(s - jnp.max(s, axis=-1, keepdims=True))
    cross_out = unstack_heads(
        dot(pltpu.roll(w, 1, 1).astype(BF16), cross[...]), jnp.sum(w, axis=-1, keepdims=True), ROWS
    )
    loads[6].wait()
    after_cross = after_self + reduce_scatter(1, dot(cross_out, wco[...]))
    x = all_gather(1, layer_norm(after_cross).astype(BF16))
    loads[7].wait()
    hidden = jnp.maximum(dot(x, wup[...]), 0.0).astype(BF16)
    loads[8].wait()
    out_ref[...] = (after_cross + reduce_scatter(2, dot(hidden, wdown[...]))).astype(BF16)

    for c in y_copies:
        c.wait_recv()
    flag_ref[0, 0] = jnp.max(jnp.maximum(jnp.maximum(flags[0], flags[1]), jnp.maximum(flags[2], flags[3])))
    for c in sent:
        c.wait_send()


def run_layer(cap, plus_hops, lengths, table, *arrays):
    lane = cap * BLK
    minus_hops = NZ - 1 - plus_hops
    keys = (SFX_HOPS + 1) * 256 + NZ * 2 * lane
    dma = pltpu.SemaphoreType.DMA
    vmem = pl.BlockSpec(memory_space=pltpu.VMEM)
    smem = pl.BlockSpec(memory_space=pltpu.SMEM)
    return pl.pallas_call(
        functools.partial(layer_kernel, cap, plus_hops),
        out_shape=(jax.ShapeDtypeStruct((SHARE, WIDTH), BF16), jax.ShapeDtypeStruct((1, 1), jnp.int32)),
        in_specs=[smem, vmem] + [pl.BlockSpec(memory_space=pltpu.HBM)] * len(arrays),
        out_specs=(vmem, smem),
        scratch_shapes=[
            pltpu.VMEM((ROWS, WIDTH), BF16),
            pltpu.VMEM((512, COLS), BF16),
            pltpu.VMEM((WIDTH, COLS), BF16),
            pltpu.VMEM((2 * WIDTH, COLS), BF16),
            pltpu.VMEM((COLS, WIDTH), BF16),
            pltpu.VMEM((WIDTH, COLS), BF16),
            pltpu.VMEM((COLS, WIDTH), BF16),
            pltpu.VMEM((WIDTH, 2048), BF16),
            pltpu.VMEM((2048, WIDTH), BF16),
            pltpu.VMEM((1024, COLS), BF16),
            pltpu.VMEM((SFX_HOPS + 1, 256, 2 * COLS), BF16),
            pltpu.VMEM((NZ, 2 * lane, 2 * COLS), BF16),
            pltpu.VMEM((NZ, 2 * lane), jnp.int32),
            pltpu.VMEM((4 * ROWS, COLS), BF16),
            pltpu.VMEM((4 * ROWS, keys), F32),
            pltpu.VMEM((3, ROWS, WIDTH), BF16),
            pltpu.VMEM((3, 4, SHARE, WIDTH), BF16),
            pltpu.VMEM((2, ROWS, WIDTH), BF16),
            pltpu.VMEM((4, 8, 256), jnp.int32),
            dma((9,)),
            dma((1,)),
            dma((4,)),
            dma((4,)),
            dma((4,)),
            dma((4,)),
            dma((1,)),
            dma((1,)),
            dma((SFX_HOPS + 1,)),
            dma((SFX_HOPS + 1,)),
            dma((SFX_HOPS + 1,)),
            dma((SFX_HOPS + 1,)),
            dma((plus_hops + 1,)),
            dma((plus_hops + 1,)),
            dma((minus_hops + 1,)),
            dma((minus_hops + 1,)),
            dma((NZ,)),
            dma((NZ,)),
            dma((3, 4)),
            dma((3, 4)),
            dma((2, 4)),
            dma((2, 4)),
        ],
        compiler_params=pltpu.CompilerParams(
            collective_id=cap // 16, has_side_effects=True, vmem_limit_bytes=56 << 20
        ),
    )(lengths, table, *arrays)


def on_device(
    tokens,
    lengths,
    block_position,
    prefix_pool,
    cross_cache,
    *weights,
):
    operands = (lengths, block_position, tokens[0], prefix_pool[0], cross_cache[0]) + weights
    out, overflow = run_layer(8, 2, *operands)
    out = lax.cond(overflow[0, 0] > 0, lambda *_: run_layer(16, 3, *operands)[0], lambda *_: out)
    return out[None]


def solution(mesh):
    return jax.shard_map(
        on_device,
        mesh=mesh,
        in_specs=(
            P("grp", "tok", None),
            P("grp", None),
            P("grp", None),
            P("grp", ("tok", "head"), None, None, None),
            P("grp", None, None, "head"),
            P(None, "head"),
            P(None, None, "head"),
            P("head", None),
            P(None, "head"),
            P("head", None),
            P(None, "head"),
            P("head", None),
        ),
        out_specs=P("grp", ("tok", "head"), None),
        check_vma=False,
    )
```

```python
import functools

import jax
import jax.numpy as jnp
from jax import lax
from jax.experimental import pallas as pl
from jax.experimental.pallas import tpu as pltpu
from jax.sharding import PartitionSpec as P

HEAD_DIM = 64
SINK = 4
WINDOW = 1024
EPS = 1e-05
MASKED = -1e30
MESH = pl.DeviceIdType.MESH

ROWS = 128
WIDTH = 1024
COLS = 256
SHARE = 32
BLK = 16
NZ = 8
SFX_HOPS = 4
PARTS = 2
F32 = jnp.float32
BF16 = jnp.bfloat16


def layer_norm(v):
    center = v - jnp.mean(v, axis=-1, keepdims=True)
    spread = jnp.mean(center * center, axis=-1, keepdims=True)
    return center * lax.rsqrt(spread + EPS)


def dot(a, b):
    return jnp.dot(a, b, preferred_element_type=F32)


def dot_t(a, b):
    return lax.dot_general(a, b, (((1,), (1,)), ((), ())), preferred_element_type=F32)


def stack_heads(q):
    head = lax.broadcasted_iota(jnp.int32, q.shape, 1) // HEAD_DIM
    zero = jnp.zeros_like(q)
    return jnp.concatenate([jnp.where(head == i, q, zero) for i in range(4)], axis=0)


def unstack_heads(summed, total, rows):
    head = lax.broadcasted_iota(jnp.int32, (rows, COLS), 1) // HEAD_DIM
    num = summed[0:rows]
    den = jnp.broadcast_to(total[0:rows], (rows, COLS))
    for i in range(1, 4):
        part = slice(i * rows, (i + 1) * rows)
        num = jnp.where(head == i, summed[part], num)
        den = jnp.where(head == i, jnp.broadcast_to(total[part], (rows, COLS)), den)
    return (num / den).astype(BF16)


def layer_kernel(
    cap,
    plus_hops,
    lengths_ref,
    table_ref,
    tokens_hbm,
    pool_hbm,
    cross_hbm,
    wq_hbm,
    wkv_hbm,
    wout_hbm,
    wcq_hbm,
    wco_hbm,
    wup_hbm,
    wdown_hbm,
    out_ref,
    flag_ref,
    tokens_ref,
    cross,
    wq,
    wkv,
    wout,
    wcq,
    wco,
    wup,
    wdown,
    raw,
    sfx,
    pk,
    places_ref,
    qbd,
    acc,
    rs_send,
    rs_recv,
    ag,
    flags,
    w_sem,
    local_sem,
    x_send,
    x_recv,
    y_send,
    y_recv,
    sib_send,
    sib_recv,
    sfx_send,
    sfx_recv,
    sfx_sib_send,
    sfx_sib_recv,
    plus_send,
    plus_recv,
    minus_send,
    minus_recv,
    pk_sib_send,
    pk_sib_recv,
    rs_s,
    rs_r,
    ag_s,
    ag_r,
):
    minus_hops = NZ - 1 - plus_hops
    lane = cap * BLK
    g = lax.axis_index("grp")
    t = lax.axis_index("tok")
    h = lax.axis_index("head")
    core = lax.rem(t, 2)
    z = t // 2
    sib = t + 1 - 2 * core
    up = lax.rem(t + 2, 2 * NZ)
    down = lax.rem(t + 2 * NZ - 2, 2 * NZ)

    def peer(r):
        return lax.rem(h + r, 4)

    def group(r):
        return lax.rem(g + r, 4)

    loads = [
        pltpu.make_async_copy(src, dst, w_sem.at[i])
        for i, (src, dst) in enumerate(
            [
                (tokens_hbm, tokens_ref),
                (wkv_hbm.reshape(2 * WIDTH, COLS), wkv),
                (wq_hbm, wq),
                (wout_hbm, wout),
                (wcq_hbm, wcq),
                (cross_hbm.reshape(512, COLS), cross),
                (wco_hbm, wco),
                (wup_hbm, wup),
                (wdown_hbm, wdown),
            ]
        )
    ]
    for c in loads[:3]:
        c.start()

    barrier = pltpu.get_barrier_semaphore()
    for dev in (
        [{"head": peer(r)} for r in (1, 2, 3)] + [{"grp": group(r)} for r in (1, 2, 3)] + [{"tok": i} for i in (sib, up, down)]
    ):
        pl.semaphore_signal(barrier, inc=1, device_id=dev, device_id_type=MESH)
    pl.semaphore_wait(barrier, 9)

    def remote(src, dst, send, recv, dev):
        return pltpu.make_async_remote_copy(
            src_ref=src, dst_ref=dst, send_sem=send, recv_sem=recv, device_id=dev, device_id_type=MESH
        )

    sent = []

    def go(c):
        c.start()
        sent.append(c)
        return c

    raw_rows = raw.at[pl.ds(pl.multiple_of(core * 512, 512) + pl.multiple_of(h * 128, 128), 128)]

    def pool_part(i):
        return pool_hbm.reshape(128, WIDTH).at[:, pl.ds(pl.multiple_of(i * COLS, COLS), COLS)]

    x_copies = [
        go(remote(pool_part(peer(r)), raw_rows, x_send.at[r], x_recv.at[r], {"head": peer(r)})) for r in (2, 1, 3)
    ]
    own_copy = pltpu.make_async_copy(pool_part(h), raw_rows, local_sem.at[0])
    own_copy.start()
    for c in loads[3:]:
        c.start()

    loads[0].wait()
    normed = layer_norm(tokens_ref[...].astype(F32)).astype(BF16)
    spread_row = lax.broadcasted_iota(jnp.int32, (128, 512), 0)
    spread_col = lax.broadcasted_iota(jnp.int32, (128, 512), 1)
    spread_to = 2 * spread_row + jnp.where(spread_col >= 256, 257, 0)
    spread = (spread_to == spread_col).astype(F32).astype(BF16)
    blocks = [normed[:, i * 128 : (i + 1) * 128] for i in range(8)]
    wide = dot(jnp.concatenate(blocks, axis=0), spread).astype(BF16)
    halves = [
        jnp.concatenate([wide[i * 128 : (i + 1) * 128, c : c + 256] for i in range(8)], axis=1) for c in (0, 256)
    ]
    my_rows = pl.ds(pl.multiple_of(core * ROWS, ROWS), ROWS)
    my_lane = pl.ds(pl.multiple_of(core * lane, lane), lane)
    loads[1].wait()
    kv = dot(jnp.concatenate(halves, axis=0), wkv[...]).astype(BF16)
    sfx[0, my_rows, 0:COLS] = kv[:ROWS]
    sfx[0, my_rows, COLS : 2 * COLS] = kv[ROWS:]

    def piece(start, rows, part):
        size = rows // PARTS
        return pl.ds(pl.multiple_of(start + part * size, size), size)

    def sfx_hop(d, part):
        rows = piece(core * ROWS, ROWS, part)
        return remote(
            sfx.at[d, rows], sfx.at[d + 1, rows], sfx_send.at[d + 1, part], sfx_recv.at[d + 1, part], {"tok": up}
        )

    def sfx_side(d):
        return remote(
            sfx.at[d, my_rows], sfx.at[d, my_rows], sfx_sib_send.at[d], sfx_sib_recv.at[d], {"tok": sib}
        )

    def plus_hop(d, part):
        rows = piece(core * lane, lane, part)
        return remote(
            pk.at[d, rows], pk.at[d + 1, rows], plus_send.at[d + 1, part], plus_recv.at[d + 1, part], {"tok": up}
        )

    def minus_hop(d, part):
        rows = piece(core * lane, lane, part)
        return remote(
            pk.at[(NZ - d) % NZ, rows],
            pk.at[NZ - d - 1, rows],
            minus_send.at[d + 1, part],
            minus_recv.at[d + 1, part],
            {"tok": down},
        )

    def pk_side(d):
        return remote(pk.at[d, my_lane], pk.at[d, my_lane], pk_sib_send.at[d], pk_sib_recv.at[d], {"tok": sib})

    hops = {"s": (sfx_hop, SFX_HOPS), "p": (plus_hop, plus_hops), "m": (minus_hop, minus_hops)}
    moving = {}
    sides = {}

    def depart(kind, d, part):
        moving[kind, d + 1, part] = go(hops[kind][0](d, part))

    def arrive(kind, d):
        if d > hops[kind][1]:
            return
        for part in range(PARTS):
            moving[kind, d, part].wait_recv()
            if d < hops[kind][1]:
                depart(kind, d, part)
        sides[kind, d] = go(sfx_side(d) if kind == "s" else pk_side(d if kind == "p" else NZ - d))

    for part in range(PARTS):
        depart("s", 0, part)
    sides["s", 0] = go(sfx_side(0))

    loads[2].wait()
    q = (dot(normed, wq[...]) * (HEAD_DIM ** -0.5)).astype(BF16)
    qbd[...] = stack_heads(q)

    table = jnp.broadcast_to(table_ref[...], (8, 256))
    needed = ((table == 0) | (table >= 192)).astype(F32)
    i0 = lax.broadcasted_iota(jnp.int32, (256, 256), 0)
    i1 = lax.broadcasted_iota(jnp.int32, (256, 256), 1)
    upto = ((i1 <= i0) & (i1 // 32 == i0 // 32)).astype(F32).astype(BF16)
    rank = dot_t(needed.astype(BF16), upto) * needed
    rank_col = dot_t(upto, needed.astype(BF16))[:, 0:1]
    flags[0] = (rank > 2 * cap).astype(jnp.int32)
    y_copies = [
        go(remote(flags.at[0], flags.at[r], y_send.at[r], y_recv.at[r], {"grp": group(r)})) for r in (1, 2, 3)
    ]
    slot_block = lax.broadcasted_iota(jnp.int32, (256, 2 * lane), 1) // BLK + 1
    held = (rank_col == slot_block.astype(F32)).astype(F32).astype(BF16)
    chip = lax.broadcasted_iota(jnp.int32, (8, 256), 1) // 32 == lax.broadcasted_iota(jnp.int32, (8, 256), 0)
    numbers = jnp.where(chip, (table + 1).astype(F32) * needed, 0.0).astype(BF16)
    places = (dot(numbers, held).astype(jnp.int32) - 1) * BLK
    places_ref[...] = places + lax.rem(lax.broadcasted_iota(jnp.int32, (8, 2 * lane), 1), BLK)
    e0 = lax.broadcasted_iota(jnp.int32, (256, 1024), 0)
    e1 = lax.broadcasted_iota(jnp.int32, (256, 1024), 1)
    enlarge = (e1 // 32 + z * 32 == e0).astype(F32).astype(BF16)
    target = (dot(rank.astype(BF16), enlarge)[0:1].astype(jnp.int32) - 1) * (2 * BLK)
    target = target + lax.rem(lax.broadcasted_iota(jnp.int32, (1, 1024), 1), 2 * BLK)
    slot = lax.broadcasted_iota(jnp.int32, (2 * lane, 1024), 0)
    slot = jnp.where(slot >= lane, 2 * (slot - lane) + 1, 2 * slot) + core * (2 * lane)
    pick = (target == slot).astype(F32).astype(BF16)

    own_copy.wait()
    for c in x_copies:
        c.wait_recv()
    half = pl.ds(pl.multiple_of(core * 512, 512), 512)
    raw_side = go(remote(raw.at[half], raw.at[half], sib_send.at[0], sib_recv.at[0], {"tok": sib}))
    arrive("s", 1)
    raw_side.wait_recv()
    packed = dot(pick, raw[...]).astype(BF16)
    pk[0, my_lane, 0:COLS] = packed[:lane]
    pk[0, my_lane, COLS : 2 * COLS] = packed[lane:]
    for part in range(PARTS):
        depart("m", 0, part)
        depart("p", 0, part)
    sides["p", 0] = go(pk_side(0))

    own_id = t * ROWS + lax.broadcasted_iota(jnp.int32, (ROWS, 256), 0)
    first = jnp.zeros((ROWS, 256), jnp.int32)
    end = jnp.int32(0)
    for i in range(8):
        length = lengths_ref[0, i]
        end = end + length
        first = first + jnp.where(own_id >= end, length, 0)
    low = jnp.maximum(first, own_id - (WINDOW - 1))
    beyond = NZ * 32 * BLK - WINDOW + own_id - first
    col = lax.broadcasted_iota(jnp.int32, (ROWS, 256), 1)

    def visible(kind, d):
        if kind == "s":
            ids = (z - d) * 256 + col
            return [(sfx, d, 0, (ids >= low) & (ids <= own_id))]
        d = d if kind == "p" else NZ - d
        row = lax.rem(z - d + NZ, NZ)
        out = []
        for j in range(2 * lane // 256):
            place = jnp.broadcast_to(places_ref[pl.ds(row, 1), j * 256 : (j + 1) * 256], (ROWS, 256))
            out.append((pk, d, j * 256, ((place >= 0) & (place < SINK)) | (place > beyond)))
        return out

    state = []

    def absorb(*chunks):
        parts = []
        for kind, d in chunks:
            if d > hops[kind][1]:
                continue
            sides[kind, d].wait_recv()
            parts += visible(kind, d)
        if not parts:
            return
        top = state[0] if state else None
        scores = []
        for buf, d, start, allowed in parts:
            s = dot_t(qbd[...], buf[d, start : start + 256, 0:COLS])
            s = jnp.where(allowed[None], s.reshape(4, ROWS, 256), MASKED).reshape(4 * ROWS, 256)
            scores.append(s)
        high = functools.reduce(jnp.maximum, [x[:, c : c + 128] for x in scores for c in (0, 128)])
        high = jnp.max(high, axis=-1, keepdims=True)
        if state:
            high = jnp.maximum(high, state[0])
            shrink = jnp.exp(state[0] - high)
            total, summed = state[1] * shrink, acc[...] * shrink
        else:
            total, summed = jnp.zeros((4 * ROWS, 128), F32), jnp.zeros((4 * ROWS, COLS), F32)
        for (buf, d, start, allowed), s in zip(parts, scores):
            w = jnp.exp(s - high)
            total = total + w[:, 0:128] + w[:, 128:256]
            summed = summed + dot(w.astype(BF16), buf[d, start : start + 256, COLS : 2 * COLS])
        acc[...] = summed
        state[:] = [high, total]

    absorb(("s", 0))
    arrive("s", 2)
    absorb(("s", 1), ("p", 0))
    arrive("m", 1)
    arrive("p", 1)
    absorb(("s", 2))
    arrive("s", 3)
    absorb(("m", 1), ("p", 1))
    arrive("m", 2)
    arrive("p", 2)
    absorb(("s", 3))
    arrive("s", 4)
    absorb(("m", 2), ("p", 2))
    arrive("m", 3)
    arrive("p", 3)
    absorb(("s", 4))
    absorb(("m", 3), ("p", 3))
    arrive("m", 4)
    absorb(("m", 4))
    attended = unstack_heads(acc[...], jnp.sum(state[1], axis=-1, keepdims=True), ROWS)

    my_share = pl.ds(pl.multiple_of(h * SHARE, SHARE), SHARE)

    def reduce_scatter(i, partial):
        rs_send[i] = partial.astype(BF16)
        copies = [
            go(
                remote(
                    rs_send.at[i, pl.ds(pl.multiple_of(peer(r) * SHARE, SHARE), SHARE)],
                    rs_recv.at[i, r],
                    rs_s.at[i, r],
                    rs_r.at[i, r],
                    {"head": peer(r)},
                )
            )
            for r in (2, 1, 3)
        ]
        total = rs_send[i, my_share, :].astype(F32)
        for c in copies:
            c.wait_recv()
        for r in (1, 2, 3):
            total = total + rs_recv[i, r].astype(F32)
        return total

    def all_gather(i, rows):
        ag[i, my_share, :] = rows
        copies = [
            go(
                remote(
                    ag.at[i, my_share], ag.at[i, my_share], ag_s.at[i, r], ag_r.at[i, r], {"head": peer(r)}
                )
            )
            for r in (2, 1, 3)
        ]
        for c in copies:
            c.wait_recv()
        return ag[i]

    loads[3].wait()
    after_self = tokens_ref[my_share, :].astype(F32) + reduce_scatter(0, dot(attended, wout[...]))
    x = all_gather(0, layer_norm(after_self).astype(BF16))
    loads[4].wait()
    cq = (dot(x, wcq[...]) * (HEAD_DIM ** -0.5)).astype(BF16)
    loads[5].wait()
    s = dot_t(stack_heads(cq), cross[...])
    is_key = lax.rem(lax.broadcasted_iota(jnp.int32, (4 * ROWS, 512), 1), 2) == 0
    s = jnp.where(is_key, s, MASKED)
    w = jnp.exp(s - jnp.max(s, axis=-1, keepdims=True))
    cross_out = unstack_heads(
        dot(pltpu.roll(w, 1, 1).astype(BF16), cross[...]), jnp.sum(w, axis=-1, keepdims=True), ROWS
    )
    loads[6].wait()
    after_cross = after_self + reduce_scatter(1, dot(cross_out, wco[...]))
    x = all_gather(1, layer_norm(after_cross).astype(BF16))
    loads[7].wait()
    hidden = jnp.maximum(dot(x, wup[...]), 0.0).astype(BF16)
    loads[8].wait()
    out_ref[...] = (after_cross + reduce_scatter(2, dot(hidden, wdown[...]))).astype(BF16)

    for c in y_copies:
        c.wait_recv()
    flag_ref[0, 0] = jnp.max(jnp.maximum(jnp.maximum(flags[0], flags[1]), jnp.maximum(flags[2], flags[3])))
    for c in sent:
        c.wait_send()


def run_layer(cap, plus_hops, lengths, table, *arrays):
    lane = cap * BLK
    minus_hops = NZ - 1 - plus_hops
    dma = pltpu.SemaphoreType.DMA
    vmem = pl.BlockSpec(memory_space=pltpu.VMEM)
    smem = pl.BlockSpec(memory_space=pltpu.SMEM)
    return pl.pallas_call(
        functools.partial(layer_kernel, cap, plus_hops),
        out_shape=(jax.ShapeDtypeStruct((SHARE, WIDTH), BF16), jax.ShapeDtypeStruct((1, 1), jnp.int32)),
        in_specs=[smem, vmem] + [pl.BlockSpec(memory_space=pltpu.HBM)] * len(arrays),
        out_specs=(vmem, smem),
        scratch_shapes=[
            pltpu.VMEM((ROWS, WIDTH), BF16),
            pltpu.VMEM((512, COLS), BF16),
            pltpu.VMEM((WIDTH, COLS), BF16),
            pltpu.VMEM((2 * WIDTH, COLS), BF16),
            pltpu.VMEM((COLS, WIDTH), BF16),
            pltpu.VMEM((WIDTH, COLS), BF16),
            pltpu.VMEM((COLS, WIDTH), BF16),
            pltpu.VMEM((WIDTH, 2048), BF16),
            pltpu.VMEM((2048, WIDTH), BF16),
            pltpu.VMEM((1024, COLS), BF16),
            pltpu.VMEM((SFX_HOPS + 1, 256, 2 * COLS), BF16),
            pltpu.VMEM((NZ, 2 * lane, 2 * COLS), BF16),
            pltpu.VMEM((NZ, 2 * lane), jnp.int32),
            pltpu.VMEM((4 * ROWS, COLS), BF16),
            pltpu.VMEM((4 * ROWS, COLS), F32),
            pltpu.VMEM((3, ROWS, WIDTH), BF16),
            pltpu.VMEM((3, 4, SHARE, WIDTH), BF16),
            pltpu.VMEM((2, ROWS, WIDTH), BF16),
            pltpu.VMEM((4, 8, 256), jnp.int32),
            dma((9,)),
            dma((1,)),
            dma((4,)),
            dma((4,)),
            dma((4,)),
            dma((4,)),
            dma((1,)),
            dma((1,)),
            dma((SFX_HOPS + 1, PARTS)),
            dma((SFX_HOPS + 1, PARTS)),
            dma((SFX_HOPS + 1,)),
            dma((SFX_HOPS + 1,)),
            dma((plus_hops + 1, PARTS)),
            dma((plus_hops + 1, PARTS)),
            dma((minus_hops + 1, PARTS)),
            dma((minus_hops + 1, PARTS)),
            dma((NZ,)),
            dma((NZ,)),
            dma((3, 4)),
            dma((3, 4)),
            dma((2, 4)),
            dma((2, 4)),
        ],
        compiler_params=pltpu.CompilerParams(
            collective_id=cap // 16, has_side_effects=True, vmem_limit_bytes=63 << 20
        ),
    )(lengths, table, *arrays)


def on_device(
    tokens,
    lengths,
    block_position,
    prefix_pool,
    cross_cache,
    *weights,
):
    operands = (lengths, block_position, tokens[0], prefix_pool[0], cross_cache[0]) + weights
    out, overflow = run_layer(8, 3, *operands)
    out = lax.cond(overflow[0, 0] > 0, lambda *_: run_layer(16, 3, *operands)[0], lambda *_: out)
    return out[None]


def solution(mesh):
    return jax.shard_map(
        on_device,
        mesh=mesh,
        in_specs=(
            P("grp", "tok", None),
            P("grp", None),
            P("grp", None),
            P("grp", ("tok", "head"), None, None, None),
            P("grp", None, None, "head"),
            P(None, "head"),
            P(None, None, "head"),
            P("head", None),
            P(None, "head"),
            P("head", None),
            P(None, "head"),
            P("head", None),
        ),
        out_specs=P("grp", ("tok", "head"), None),
        check_vma=False,
    )
```

```python
import functools

import jax
import jax.numpy as jnp
from jax import lax
from jax.experimental import pallas as pl
from jax.experimental.pallas import tpu as pltpu
from jax.sharding import PartitionSpec as P

HEAD_DIM = 64
SINK = 4
WINDOW = 1024
EPS = 1e-05
MASKED = -1e30
MESH = pl.DeviceIdType.MESH

ROWS = 128
WIDTH = 1024
COLS = 256
SHARE = 32
BLK = 16
NZ = 8
SFX_HOPS = 4
PARTS = 2
F32 = jnp.float32
BF16 = jnp.bfloat16


def layer_norm(v):
    center = v - jnp.mean(v, axis=-1, keepdims=True)
    spread = jnp.mean(center * center, axis=-1, keepdims=True)
    return center * lax.rsqrt(spread + EPS)


def dot(a, b):
    return jnp.dot(a, b, preferred_element_type=F32)


def dot_t(a, b):
    return lax.dot_general(a, b, (((1,), (1,)), ((), ())), preferred_element_type=F32)


def stack_heads(q):
    head = lax.broadcasted_iota(jnp.int32, q.shape, 1) // HEAD_DIM
    zero = jnp.zeros_like(q)
    return jnp.concatenate([jnp.where(head == i, q, zero) for i in range(4)], axis=0)


def unstack_heads(summed, total, rows):
    head = lax.broadcasted_iota(jnp.int32, (rows, COLS), 1) // HEAD_DIM
    num = summed[0:rows]
    den = jnp.broadcast_to(total[0:rows], (rows, COLS))
    for i in range(1, 4):
        part = slice(i * rows, (i + 1) * rows)
        num = jnp.where(head == i, summed[part], num)
        den = jnp.where(head == i, jnp.broadcast_to(total[part], (rows, COLS)), den)
    return (num / den).astype(BF16)


def layer_kernel(
    cap,
    plus_hops,
    lengths_ref,
    table_ref,
    tokens_hbm,
    pool_hbm,
    cross_hbm,
    wq_hbm,
    wkv_hbm,
    wout_hbm,
    wcq_hbm,
    wco_hbm,
    wup_hbm,
    wdown_hbm,
    out_ref,
    flag_ref,
    tokens_ref,
    cross,
    wq,
    wkv,
    wout,
    wcq,
    wco,
    wup,
    wdown,
    raw,
    cross_raw,
    sfx,
    pk,
    places_ref,
    qbd,
    acc,
    at_send,
    at_recv,
    rs_send,
    rs_recv,
    ag,
    flags,
    w_sem,
    local_sem,
    x_send,
    x_recv,
    y_send,
    y_recv,
    sib_send,
    sib_recv,
    sfx_send,
    sfx_recv,
    sfx_sib_send,
    sfx_sib_recv,
    plus_send,
    plus_recv,
    minus_send,
    minus_recv,
    pk_sib_send,
    pk_sib_recv,
    at_s,
    at_r,
    rs_s,
    rs_r,
    ag_s,
    ag_r,
    wx_s,
    wx_r,
    wy_s,
    wy_r,
    wz_s,
    wz_r,
    cx_s,
    cx_r,
    cz_s,
    cz_r,
):
    minus_hops = NZ - 1 - plus_hops
    lane = cap * BLK
    g = lax.axis_index("grp")
    t = lax.axis_index("tok")
    h = lax.axis_index("head")
    core = lax.rem(t, 2)
    z = t // 2
    sib = t + 1 - 2 * core
    up = lax.rem(t + 2, 2 * NZ)
    down = lax.rem(t + 2 * NZ - 2, 2 * NZ)

    def peer(r):
        return lax.rem(h + r, 4)

    def group(r):
        return lax.rem(g + r, 4)

    loads = [
        pltpu.make_async_copy(src, dst, w_sem.at[i])
        for i, (src, dst) in enumerate(
            [
                (tokens_hbm, tokens_ref),
                (wkv_hbm.reshape(2 * WIDTH, COLS), wkv),
                (wq_hbm, wq),
                (cross_hbm.reshape(512, COLS), cross_raw),
                (wout_hbm, wout.at[h]),
                (wcq_hbm, wcq.at[h]),
                (wco_hbm, wco.at[h]),
                (wup_hbm, wup),
                (wdown_hbm, wdown),
            ]
        )
    ]
    for c in loads[:3]:
        c.start()

    barrier = pltpu.get_barrier_semaphore()
    for dev in (
        [{"head": peer(r)} for r in (1, 2, 3)] + [{"grp": group(r)} for r in (1, 2, 3)] + [{"tok": i} for i in (sib, up, down)]
    ):
        pl.semaphore_signal(barrier, inc=1, device_id=dev, device_id_type=MESH)
    pl.semaphore_wait(barrier, 9)

    def remote(src, dst, send, recv, dev):
        return pltpu.make_async_remote_copy(
            src_ref=src, dst_ref=dst, send_sem=send, recv_sem=recv, device_id=dev, device_id_type=MESH
        )

    sent = []

    def go(c):
        c.start()
        sent.append(c)
        return c

    raw_rows = raw.at[pl.ds(pl.multiple_of(core * 512, 512) + pl.multiple_of(h * 128, 128), 128)]

    def pool_part(i):
        return pool_hbm.reshape(128, WIDTH).at[:, pl.ds(pl.multiple_of(i * COLS, COLS), COLS)]

    x_copies = [
        go(remote(pool_part(peer(r)), raw_rows, x_send.at[r], x_recv.at[r], {"head": peer(r)})) for r in (2, 1, 3)
    ]
    own_copy = pltpu.make_async_copy(pool_part(h), raw_rows, local_sem.at[0])
    own_copy.start()
    for c in loads[3:]:
        c.start()

    loads[0].wait()
    normed = layer_norm(tokens_ref[...].astype(F32)).astype(BF16)
    spread_row = lax.broadcasted_iota(jnp.int32, (128, 512), 0)
    spread_col = lax.broadcasted_iota(jnp.int32, (128, 512), 1)
    spread_to = 2 * spread_row + jnp.where(spread_col >= 256, 257, 0)
    spread = (spread_to == spread_col).astype(F32).astype(BF16)
    blocks = [normed[:, i * 128 : (i + 1) * 128] for i in range(8)]
    wide = dot(jnp.concatenate(blocks, axis=0), spread).astype(BF16)
    halves = [
        jnp.concatenate([wide[i * 128 : (i + 1) * 128, c : c + 256] for i in range(8)], axis=1) for c in (0, 256)
    ]
    my_rows = pl.ds(pl.multiple_of(core * ROWS, ROWS), ROWS)
    my_lane = pl.ds(pl.multiple_of(core * lane, lane), lane)
    loads[1].wait()
    kv = dot(jnp.concatenate(halves, axis=0), wkv[...]).astype(BF16)
    sfx[0, my_rows, 0:COLS] = kv[:ROWS]
    sfx[0, my_rows, COLS : 2 * COLS] = kv[ROWS:]

    def piece(start, rows, part):
        size = rows // PARTS
        return pl.ds(pl.multiple_of(start + part * size, size), size)

    def sfx_hop(d, part):
        rows = piece(core * ROWS, ROWS, part)
        return remote(
            sfx.at[d, rows], sfx.at[d + 1, rows], sfx_send.at[d + 1, part], sfx_recv.at[d + 1, part], {"tok": up}
        )

    def sfx_side(d):
        return remote(
            sfx.at[d, my_rows], sfx.at[d, my_rows], sfx_sib_send.at[d], sfx_sib_recv.at[d], {"tok": sib}
        )

    def plus_hop(d, part):
        rows = piece(core * lane, lane, part)
        return remote(
            pk.at[d, rows], pk.at[d + 1, rows], plus_send.at[d + 1, part], plus_recv.at[d + 1, part], {"tok": up}
        )

    def minus_hop(d, part):
        rows = piece(core * lane, lane, part)
        return remote(
            pk.at[(NZ - d) % NZ, rows],
            pk.at[NZ - d - 1, rows],
            minus_send.at[d + 1, part],
            minus_recv.at[d + 1, part],
            {"tok": down},
        )

    def pk_side(d):
        return remote(pk.at[d, my_lane], pk.at[d, my_lane], pk_sib_send.at[d], pk_sib_recv.at[d], {"tok": sib})

    hops = {"s": (sfx_hop, SFX_HOPS), "p": (plus_hop, plus_hops), "m": (minus_hop, minus_hops)}
    moving = {}
    sides = {}

    def depart(kind, d, part):
        moving[kind, d + 1, part] = go(hops[kind][0](d, part))

    def arrive(kind, d):
        if d > hops[kind][1]:
            return
        for part in range(PARTS):
            moving[kind, d, part].wait_recv()
            if d < hops[kind][1]:
                depart(kind, d, part)
        sides[kind, d] = go(sfx_side(d) if kind == "s" else pk_side(d if kind == "p" else NZ - d))

    for part in range(PARTS):
        depart("s", 0, part)
    sides["s", 0] = go(sfx_side(0))

    shared = [wout, wcq, wco]
    eighth = core * 4 + g

    def shard(r):
        return lax.rem(h + 4 - r, 4)

    def held_rows(i):
        size = shared[i].shape[1] // 8
        return pl.ds(pl.multiple_of(eighth * size, size), size)

    weights_x, weights_y, weights_z, cross_x, cross_z = {}, {}, {}, {}, {}

    def weights_start(i):
        loads[4 + i].wait()
        part = shared[i].at[h, held_rows(i)]
        for r in (1, 3, 2):
            weights_x[i, r] = go(remote(part, part, wx_s.at[i, r], wx_r.at[i, r], {"head": peer(r)}))

    def weights_share(i):
        for r in (1, 3, 2):
            weights_x[i, r].wait_recv()
            part = shared[i].at[shard(r), held_rows(i)]
            for q in (1, 3, 2):
                weights_y[i, r, q] = go(remote(part, part, wy_s.at[i, r, q], wy_r.at[i, r, q], {"grp": group(q)}))

    def weights_pass(i):
        size = shared[i].shape[1] // 2
        for r in (1, 3, 2):
            for q in (1, 3, 2):
                weights_y[i, r, q].wait_recv()
            part = shared[i].at[shard(r), pl.ds(pl.multiple_of(core * size, size), size)]
            weights_z[i, r] = go(remote(part, part, wz_s.at[i, r], wz_r.at[i, r], {"tok": sib}))

    def weights_done(i):
        for r in (1, 3, 2):
            weights_z[i, r].wait_recv()

    for i in range(3):
        weights_start(i)
    d0 = lax.broadcasted_iota(jnp.int32, (512, 512), 0)
    d1 = lax.broadcasted_iota(jnp.int32, (512, 512), 1)
    split = (jnp.where(d0 >= 256, 2 * d0 - 511, 2 * d0) == d1).astype(F32).astype(BF16)
    loads[3].wait()
    cross[h] = dot(split, cross_raw[...]).astype(BF16)
    cross_rows = pl.ds(pl.multiple_of(core * 256, 256), 256)
    for r in (1, 3, 2):
        part = cross.at[h, cross_rows]
        cross_x[r] = go(remote(part, part, cx_s.at[r], cx_r.at[r], {"head": peer(r)}))

    def cross_pass():
        for r in (1, 3, 2):
            cross_x[r].wait_recv()
            part = cross.at[shard(r), cross_rows]
            cross_z[r] = go(remote(part, part, cz_s.at[r], cz_r.at[r], {"tok": sib}))

    loads[2].wait()
    q = (dot(normed, wq[...]) * (HEAD_DIM ** -0.5)).astype(BF16)
    qbd[...] = stack_heads(q)

    table = jnp.broadcast_to(table_ref[...], (8, 256))
    needed = ((table == 0) | (table >= 192)).astype(F32)
    i0 = lax.broadcasted_iota(jnp.int32, (256, 256), 0)
    i1 = lax.broadcasted_iota(jnp.int32, (256, 256), 1)
    upto = ((i1 <= i0) & (i1 // 32 == i0 // 32)).astype(F32).astype(BF16)
    rank = dot_t(needed.astype(BF16), upto) * needed
    rank_col = dot_t(upto, needed.astype(BF16))[:, 0:1]
    flags[0] = (rank > 2 * cap).astype(jnp.int32)
    y_copies = [
        go(remote(flags.at[0], flags.at[r], y_send.at[r], y_recv.at[r], {"grp": group(r)})) for r in (1, 2, 3)
    ]
    slot_block = lax.broadcasted_iota(jnp.int32, (256, 2 * lane), 1) // BLK + 1
    held = (rank_col == slot_block.astype(F32)).astype(F32).astype(BF16)
    chip = lax.broadcasted_iota(jnp.int32, (8, 256), 1) // 32 == lax.broadcasted_iota(jnp.int32, (8, 256), 0)
    numbers = jnp.where(chip, (table + 1).astype(F32) * needed, 0.0).astype(BF16)
    places = (dot(numbers, held).astype(jnp.int32) - 1) * BLK
    places_ref[...] = places + lax.rem(lax.broadcasted_iota(jnp.int32, (8, 2 * lane), 1), BLK)
    e0 = lax.broadcasted_iota(jnp.int32, (256, 1024), 0)
    e1 = lax.broadcasted_iota(jnp.int32, (256, 1024), 1)
    enlarge = (e1 // 32 + z * 32 == e0).astype(F32).astype(BF16)
    target = (dot(rank.astype(BF16), enlarge)[0:1].astype(jnp.int32) - 1) * (2 * BLK)
    target = target + lax.rem(lax.broadcasted_iota(jnp.int32, (1, 1024), 1), 2 * BLK)
    slot = lax.broadcasted_iota(jnp.int32, (2 * lane, 1024), 0)
    slot = jnp.where(slot >= lane, 2 * (slot - lane) + 1, 2 * slot) + core * (2 * lane)
    pick = (target == slot).astype(F32).astype(BF16)

    own_copy.wait()
    for c in x_copies:
        c.wait_recv()
    half = pl.ds(pl.multiple_of(core * 512, 512), 512)
    raw_side = go(remote(raw.at[half], raw.at[half], sib_send.at[0], sib_recv.at[0], {"tok": sib}))
    arrive("s", 1)
    raw_side.wait_recv()
    packed = dot(pick, raw[...]).astype(BF16)
    pk[0, my_lane, 0:COLS] = packed[:lane]
    pk[0, my_lane, COLS : 2 * COLS] = packed[lane:]
    for part in range(PARTS):
        depart("m", 0, part)
        depart("p", 0, part)
    sides["p", 0] = go(pk_side(0))

    own_id = t * ROWS + lax.broadcasted_iota(jnp.int32, (ROWS, 256), 0)
    first = jnp.zeros((ROWS, 256), jnp.int32)
    end = jnp.int32(0)
    for i in range(8):
        length = lengths_ref[0, i]
        end = end + length
        first = first + jnp.where(own_id >= end, length, 0)
    low = jnp.maximum(first, own_id - (WINDOW - 1))
    beyond = NZ * 32 * BLK - WINDOW + own_id - first
    col = lax.broadcasted_iota(jnp.int32, (ROWS, 256), 1)

    def visible(kind, d):
        if kind == "s":
            ids = (z - d) * 256 + col
            return [(sfx, d, 0, (ids >= low) & (ids <= own_id))]
        d = d if kind == "p" else NZ - d
        row = lax.rem(z - d + NZ, NZ)
        out = []
        for j in range(2 * lane // 256):
            place = jnp.broadcast_to(places_ref[pl.ds(row, 1), j * 256 : (j + 1) * 256], (ROWS, 256))
            out.append((pk, d, j * 256, ((place >= 0) & (place < SINK)) | (place > beyond)))
        return out

    state = []

    def absorb(*chunks):
        parts = []
        for kind, d in chunks:
            if d > hops[kind][1]:
                continue
            sides[kind, d].wait_recv()
            parts += visible(kind, d)
        if not parts:
            return
        top = state[0] if state else None
        scores = []
        for buf, d, start, allowed in parts:
            s = dot_t(qbd[...], buf[d, start : start + 256, 0:COLS])
            s = jnp.where(allowed[None], s.reshape(4, ROWS, 256), MASKED).reshape(4 * ROWS, 256)
            scores.append(s)
        high = functools.reduce(jnp.maximum, [x[:, c : c + 128] for x in scores for c in (0, 128)])
        high = jnp.max(high, axis=-1, keepdims=True)
        if state:
            high = jnp.maximum(high, state[0])
            shrink = jnp.exp(state[0] - high)
            total, summed = state[1] * shrink, acc[...] * shrink
        else:
            total, summed = jnp.zeros((4 * ROWS, 128), F32), jnp.zeros((4 * ROWS, COLS), F32)
        for (buf, d, start, allowed), s in zip(parts, scores):
            w = jnp.exp(s - high)
            total = total + w[:, 0:128] + w[:, 128:256]
            summed = summed + dot(w.astype(BF16), buf[d, start : start + 256, COLS : 2 * COLS])
        acc[...] = summed
        state[:] = [high, total]

    absorb(("s", 0))
    arrive("s", 2)
    absorb(("s", 1), ("p", 0))
    weights_share(0)
    arrive("m", 1)
    arrive("p", 1)
    absorb(("s", 2))
    arrive("s", 3)
    weights_share(1)
    absorb(("m", 1), ("p", 1))
    arrive("m", 2)
    arrive("p", 2)
    absorb(("s", 3))
    arrive("s", 4)
    weights_share(2)
    absorb(("m", 2), ("p", 2))
    arrive("m", 3)
    arrive("p", 3)
    cross_pass()
    weights_pass(0)
    absorb(("s", 4))
    absorb(("m", 3), ("p", 3))
    arrive("m", 4)
    absorb(("m", 4))
    attended = unstack_heads(acc[...], jnp.sum(state[1], axis=-1, keepdims=True), ROWS)

    my_share = pl.ds(pl.multiple_of(h * SHARE, SHARE), SHARE)

    def reduce_scatter(i, partial):
        rs_send[i] = partial.astype(BF16)
        copies = [
            go(
                remote(
                    rs_send.at[i, pl.ds(pl.multiple_of(peer(r) * SHARE, SHARE), SHARE)],
                    rs_recv.at[i, r],
                    rs_s.at[i, r],
                    rs_r.at[i, r],
                    {"head": peer(r)},
                )
            )
            for r in (2, 1, 3)
        ]
        total = rs_send[i, my_share, :].astype(F32)
        for c in copies:
            c.wait_recv()
        for r in (1, 2, 3):
            total = total + rs_recv[i, r].astype(F32)
        return total

    def all_gather(i, rows):
        ag[i, my_share, :] = rows
        copies = [
            go(
                remote(
                    ag.at[i, my_share], ag.at[i, my_share], ag_s.at[i, r], ag_r.at[i, r], {"head": peer(r)}
                )
            )
            for r in (2, 1, 3)
        ]
        for c in copies:
            c.wait_recv()
        return ag[i]

    at_send[...] = attended
    at_copies = [
        go(
            remote(
                at_send.at[pl.ds(pl.multiple_of(peer(r) * SHARE, SHARE), SHARE)],
                at_recv.at[h],
                at_s.at[r],
                at_r.at[r],
                {"head": peer(r)},
            )
        )
        for r in (2, 1, 3)
    ]
    at_recv[h] = at_send[my_share, :]
    weights_pass(1)
    weights_done(0)
    for c in at_copies:
        c.wait_recv()
    after_self = tokens_ref[my_share, :].astype(F32) + sum(dot(at_recv[i], wout[i]) for i in range(4))
    x = layer_norm(after_self).astype(BF16)
    weights_pass(2)
    weights_done(1)
    for r in (1, 3, 2):
        cross_z[r].wait_recv()
    outs = []
    for i in range(4):
        cq = (dot(x, wcq[i]) * (HEAD_DIM ** -0.5)).astype(BF16)
        s = dot_t(stack_heads(cq), cross[i, 0:256])
        w = jnp.exp(s - jnp.max(s, axis=-1, keepdims=True))
        outs.append(
            unstack_heads(dot(w.astype(BF16), cross[i, 256:512]), jnp.sum(w, axis=-1, keepdims=True), SHARE)
        )
    weights_done(2)
    after_cross = after_self + sum(dot(outs[i], wco[i]) for i in range(4))
    x = all_gather(0, layer_norm(after_cross).astype(BF16))
    loads[7].wait()
    hidden = jnp.maximum(dot(x, wup[...]), 0.0).astype(BF16)
    loads[8].wait()
    out_ref[...] = (after_cross + reduce_scatter(0, dot(hidden, wdown[...]))).astype(BF16)

    for c in y_copies:
        c.wait_recv()
    flag_ref[0, 0] = jnp.max(jnp.maximum(jnp.maximum(flags[0], flags[1]), jnp.maximum(flags[2], flags[3])))
    for c in sent:
        c.wait_send()


def run_layer(cap, plus_hops, lengths, table, *arrays):
    lane = cap * BLK
    minus_hops = NZ - 1 - plus_hops
    dma = pltpu.SemaphoreType.DMA
    vmem = pl.BlockSpec(memory_space=pltpu.VMEM)
    smem = pl.BlockSpec(memory_space=pltpu.SMEM)
    return pl.pallas_call(
        functools.partial(layer_kernel, cap, plus_hops),
        out_shape=(jax.ShapeDtypeStruct((SHARE, WIDTH), BF16), jax.ShapeDtypeStruct((1, 1), jnp.int32)),
        in_specs=[smem, vmem] + [pl.BlockSpec(memory_space=pltpu.HBM)] * len(arrays),
        out_specs=(vmem, smem),
        scratch_shapes=[
            pltpu.VMEM((ROWS, WIDTH), BF16),
            pltpu.VMEM((4, 512, COLS), BF16),
            pltpu.VMEM((WIDTH, COLS), BF16),
            pltpu.VMEM((2 * WIDTH, COLS), BF16),
            pltpu.VMEM((4, COLS, WIDTH), BF16),
            pltpu.VMEM((4, WIDTH, COLS), BF16),
            pltpu.VMEM((4, COLS, WIDTH), BF16),
            pltpu.VMEM((WIDTH, 2048), BF16),
            pltpu.VMEM((2048, WIDTH), BF16),
            pltpu.VMEM((1024, COLS), BF16),
            pltpu.VMEM((512, COLS), BF16),
            pltpu.VMEM((SFX_HOPS + 1, 256, 2 * COLS), BF16),
            pltpu.VMEM((NZ, 2 * lane, 2 * COLS), BF16),
            pltpu.VMEM((NZ, 2 * lane), jnp.int32),
            pltpu.VMEM((4 * ROWS, COLS), BF16),
            pltpu.VMEM((4 * ROWS, COLS), F32),
            pltpu.VMEM((ROWS, COLS), BF16),
            pltpu.VMEM((4, SHARE, COLS), BF16),
            pltpu.VMEM((1, ROWS, WIDTH), BF16),
            pltpu.VMEM((1, 4, SHARE, WIDTH), BF16),
            pltpu.VMEM((1, ROWS, WIDTH), BF16),
            pltpu.VMEM((4, 8, 256), jnp.int32),
            dma((9,)),
            dma((1,)),
            dma((4,)),
            dma((4,)),
            dma((4,)),
            dma((4,)),
            dma((1,)),
            dma((1,)),
            dma((SFX_HOPS + 1, PARTS)),
            dma((SFX_HOPS + 1, PARTS)),
            dma((SFX_HOPS + 1,)),
            dma((SFX_HOPS + 1,)),
            dma((plus_hops + 1, PARTS)),
            dma((plus_hops + 1, PARTS)),
            dma((minus_hops + 1, PARTS)),
            dma((minus_hops + 1, PARTS)),
            dma((NZ,)),
            dma((NZ,)),
            dma((4,)),
            dma((4,)),
            dma((1, 4)),
            dma((1, 4)),
            dma((1, 4)),
            dma((1, 4)),
            dma((3, 4)),
            dma((3, 4)),
            dma((3, 4, 4)),
            dma((3, 4, 4)),
            dma((3, 4)),
            dma((3, 4)),
            dma((4,)),
            dma((4,)),
            dma((4,)),
            dma((4,)),
        ],
        compiler_params=pltpu.CompilerParams(
            collective_id=cap // 16, has_side_effects=True, vmem_limit_bytes=63 << 20
        ),
    )(lengths, table, *arrays)


def on_device(
    tokens,
    lengths,
    block_position,
    prefix_pool,
    cross_cache,
    *weights,
):
    operands = (lengths, block_position, tokens[0], prefix_pool[0], cross_cache[0]) + weights
    out, overflow = run_layer(8, 3, *operands)
    out = lax.cond(overflow[0, 0] > 0, lambda *_: run_layer(16, 3, *operands)[0], lambda *_: out)
    return out[None]


def solution(mesh):
    return jax.shard_map(
        on_device,
        mesh=mesh,
        in_specs=(
            P("grp", "tok", None),
            P("grp", None),
            P("grp", None),
            P("grp", ("tok", "head"), None, None, None),
            P("grp", None, None, "head"),
            P(None, "head"),
            P(None, None, "head"),
            P("head", None),
            P(None, "head"),
            P("head", None),
            P(None, "head"),
            P("head", None),
        ),
        out_specs=P("grp", ("tok", "head"), None),
        check_vma=False,
    )
```

```python
import functools

import jax
import jax.numpy as jnp
from jax import lax
from jax.experimental import pallas as pl
from jax.experimental.pallas import tpu as pltpu
from jax.sharding import PartitionSpec as P

HEAD_DIM = 64
SINK = 4
WINDOW = 1024
EPS = 1e-05
MASKED = -1e30
MESH = pl.DeviceIdType.MESH

ROWS = 128
WIDTH = 1024
COLS = 256
SHARE = 32
BLK = 16
NZ = 8
SFX_HOPS = 4
F32 = jnp.float32
BF16 = jnp.bfloat16


def layer_norm(v):
    center = v - jnp.mean(v, axis=-1, keepdims=True)
    spread = jnp.mean(center * center, axis=-1, keepdims=True)
    return center * lax.rsqrt(spread + EPS)


def dot(a, b):
    return jnp.dot(a, b, preferred_element_type=F32)


def dot_t(a, b):
    return lax.dot_general(a, b, (((1,), (1,)), ((), ())), preferred_element_type=F32)


def stack_heads(q):
    head = lax.broadcasted_iota(jnp.int32, q.shape, 1) // HEAD_DIM
    zero = jnp.zeros_like(q)
    return jnp.concatenate([jnp.where(head == i, q, zero) for i in range(4)], axis=0)


def unstack_heads(summed, total, rows):
    head = lax.broadcasted_iota(jnp.int32, (rows, COLS), 1) // HEAD_DIM
    num = summed[0:rows]
    den = jnp.broadcast_to(total[0:rows], (rows, COLS))
    for i in range(1, 4):
        part = slice(i * rows, (i + 1) * rows)
        num = jnp.where(head == i, summed[part], num)
        den = jnp.where(head == i, jnp.broadcast_to(total[part], (rows, COLS)), den)
    return (num / den).astype(BF16)


def layer_kernel(
    cap,
    plus_hops,
    parts,
    lengths_ref,
    table_ref,
    tokens_hbm,
    pool_hbm,
    cross_hbm,
    wq_hbm,
    wkv_hbm,
    wout_hbm,
    wcq_hbm,
    wco_hbm,
    wup_hbm,
    wdown_hbm,
    out_ref,
    flag_ref,
    tokens_ref,
    cross,
    wq,
    wkv,
    wout,
    wcq,
    wco,
    wup,
    wdown,
    pool,
    raw,
    cross_raw,
    sfx,
    pk,
    places_ref,
    qbd,
    acc,
    at_send,
    at_recv,
    rs_send,
    rs_recv,
    ag,
    flags,
    w_sem,
    local_sem,
    x_send,
    x_recv,
    y_send,
    y_recv,
    sib_send,
    sib_recv,
    sfx_send,
    sfx_recv,
    sfx_sib_send,
    sfx_sib_recv,
    plus_send,
    plus_recv,
    minus_send,
    minus_recv,
    pk_sib_send,
    pk_sib_recv,
    at_s,
    at_r,
    rs_s,
    rs_r,
    ag_s,
    ag_r,
    wx_s,
    wx_r,
    wy_s,
    wy_r,
    wz_s,
    wz_r,
    cx_s,
    cx_r,
    cz_s,
    cz_r,
):
    minus_hops = NZ - 1 - plus_hops
    lane = cap * BLK
    g = lax.axis_index("grp")
    t = lax.axis_index("tok")
    h = lax.axis_index("head")
    core = lax.rem(t, 2)
    z = t // 2
    sib = t + 1 - 2 * core
    up = lax.rem(t + 2, 2 * NZ)
    down = lax.rem(t + 2 * NZ - 2, 2 * NZ)

    def peer(r):
        return lax.rem(h + r, 4)

    def group(r):
        return lax.rem(g + r, 4)

    loads = [
        pltpu.make_async_copy(src, dst, w_sem.at[i])
        for i, (src, dst) in enumerate(
            [
                (tokens_hbm, tokens_ref),
                (wkv_hbm.reshape(2 * WIDTH, COLS), wkv),
                (wq_hbm, wq),
                (cross_hbm.reshape(512, COLS), cross_raw),
                (wout_hbm, wout.at[h]),
                (wcq_hbm, wcq.at[h]),
                (wco_hbm, wco.at[h]),
                (wup_hbm, wup),
                (wdown_hbm, wdown),
            ]
        )
    ]
    pool_copy = pltpu.make_async_copy(pool_hbm.reshape(128, WIDTH), pool, local_sem.at[1])
    pool_copy.start()
    for c in loads[:3]:
        c.start()

    barrier = pltpu.get_barrier_semaphore()
    for dev in (
        [{"head": peer(r)} for r in (1, 2, 3)] + [{"grp": group(r)} for r in (1, 2, 3)] + [{"tok": i} for i in (sib, up, down)]
    ):
        pl.semaphore_signal(barrier, inc=1, device_id=dev, device_id_type=MESH)
    pl.semaphore_wait(barrier, 9)

    def remote(src, dst, send, recv, dev):
        return pltpu.make_async_remote_copy(
            src_ref=src, dst_ref=dst, send_sem=send, recv_sem=recv, device_id=dev, device_id_type=MESH
        )

    sent = []

    def go(c):
        c.start()
        sent.append(c)
        return c

    raw_rows = raw.at[pl.ds(pl.multiple_of(core * 512, 512) + pl.multiple_of(h * 128, 128), 128)]

    def pool_part(i):
        return pool.at[:, pl.ds(pl.multiple_of(i * COLS, COLS), COLS)]

    pool_copy.wait()
    x_copies = [
        go(remote(pool_part(peer(r)), raw_rows, x_send.at[r], x_recv.at[r], {"head": peer(r)})) for r in (2, 1, 3)
    ]
    own_copy = pltpu.make_async_copy(pool_part(h), raw_rows, local_sem.at[0])
    own_copy.start()
    for c in loads[3:7]:
        c.start()

    loads[0].wait()
    normed = layer_norm(tokens_ref[...].astype(F32)).astype(BF16)
    spread_row = lax.broadcasted_iota(jnp.int32, (128, 512), 0)
    spread_col = lax.broadcasted_iota(jnp.int32, (128, 512), 1)
    spread_to = 2 * spread_row + jnp.where(spread_col >= 256, 257, 0)
    spread = (spread_to == spread_col).astype(F32).astype(BF16)
    blocks = [normed[:, i * 128 : (i + 1) * 128] for i in range(8)]
    wide = dot(jnp.concatenate(blocks, axis=0), spread).astype(BF16)
    halves = [
        jnp.concatenate([wide[i * 128 : (i + 1) * 128, c : c + 256] for i in range(8)], axis=1) for c in (0, 256)
    ]
    my_rows = pl.ds(pl.multiple_of(core * ROWS, ROWS), ROWS)
    my_lane = pl.ds(pl.multiple_of(core * lane, lane), lane)
    loads[1].wait()
    kv = dot(jnp.concatenate(halves, axis=0), wkv[...]).astype(BF16)
    sfx[0, my_rows, 0:COLS] = kv[:ROWS]
    sfx[0, my_rows, COLS : 2 * COLS] = kv[ROWS:]

    def piece(start, rows, part):
        size = rows // parts
        return pl.ds(pl.multiple_of(start + part * size, size), size)

    def sfx_hop(d, part):
        rows = piece(core * ROWS, ROWS, part)
        return remote(
            sfx.at[d, rows], sfx.at[d + 1, rows], sfx_send.at[d + 1, part], sfx_recv.at[d + 1, part], {"tok": up}
        )

    def sfx_side(d):
        return remote(
            sfx.at[d, my_rows], sfx.at[d, my_rows], sfx_sib_send.at[d], sfx_sib_recv.at[d], {"tok": sib}
        )

    def plus_hop(d, part):
        rows = piece(core * lane, lane, part)
        return remote(
            pk.at[d, rows], pk.at[d + 1, rows], plus_send.at[d + 1, part], plus_recv.at[d + 1, part], {"tok": up}
        )

    def minus_hop(d, part):
        rows = piece(core * lane, lane, part)
        return remote(
            pk.at[(NZ - d) % NZ, rows],
            pk.at[NZ - d - 1, rows],
            minus_send.at[d + 1, part],
            minus_recv.at[d + 1, part],
            {"tok": down},
        )

    def pk_side(d):
        return remote(pk.at[d, my_lane], pk.at[d, my_lane], pk_sib_send.at[d], pk_sib_recv.at[d], {"tok": sib})

    hops = {"s": (sfx_hop, SFX_HOPS), "p": (plus_hop, plus_hops), "m": (minus_hop, minus_hops)}
    moving = {}
    sides = {}

    def depart(kind, d, part):
        moving[kind, d + 1, part] = go(hops[kind][0](d, part))

    def arrive(kind, d):
        if d > hops[kind][1]:
            return
        for part in range(parts):
            moving[kind, d, part].wait_recv()
            if d < hops[kind][1]:
                depart(kind, d, part)
        sides[kind, d] = go(sfx_side(d) if kind == "s" else pk_side(d if kind == "p" else NZ - d))

    for part in range(parts):
        depart("s", 0, part)
    sides["s", 0] = go(sfx_side(0))

    shared = [wout, wcq, wco]
    eighth = core * 4 + g

    def shard(r):
        return lax.rem(h + 4 - r, 4)

    def held_rows(i):
        size = shared[i].shape[1] // 8
        return pl.ds(pl.multiple_of(eighth * size, size), size)

    weights_x, weights_y, weights_z, cross_x, cross_z = {}, {}, {}, {}, {}

    def weights_start(i):
        loads[4 + i].wait()
        part = shared[i].at[h, held_rows(i)]
        for r in (1, 3, 2):
            weights_x[i, r] = go(remote(part, part, wx_s.at[i, r], wx_r.at[i, r], {"head": peer(r)}))

    def weights_share(i):
        for r in (1, 3, 2):
            weights_x[i, r].wait_recv()
            part = shared[i].at[shard(r), held_rows(i)]
            for q in (1, 3, 2):
                weights_y[i, r, q] = go(remote(part, part, wy_s.at[i, r, q], wy_r.at[i, r, q], {"grp": group(q)}))

    def weights_pass(i):
        size = shared[i].shape[1] // 2
        for r in (1, 3, 2):
            for q in (1, 3, 2):
                weights_y[i, r, q].wait_recv()
            part = shared[i].at[shard(r), pl.ds(pl.multiple_of(core * size, size), size)]
            weights_z[i, r] = go(remote(part, part, wz_s.at[i, r], wz_r.at[i, r], {"tok": sib}))

    def weights_done(i):
        for r in (1, 3, 2):
            weights_z[i, r].wait_recv()

    cross_rows = pl.ds(pl.multiple_of(core * 256, 256), 256)

    def cross_start():
        for r in (1, 3, 2):
            part = cross.at[h, cross_rows]
            cross_x[r] = go(remote(part, part, cx_s.at[r], cx_r.at[r], {"head": peer(r)}))

    def cross_pass():
        for r in (1, 3, 2):
            cross_x[r].wait_recv()
            part = cross.at[shard(r), cross_rows]
            cross_z[r] = go(remote(part, part, cz_s.at[r], cz_r.at[r], {"tok": sib}))

    loads[2].wait()
    q = (dot(normed, wq[...]) * (HEAD_DIM ** -0.5)).astype(BF16)
    qbd[...] = stack_heads(q)

    table = jnp.broadcast_to(table_ref[...], (8, 256))
    needed = ((table == 0) | (table >= 192)).astype(F32)
    i0 = lax.broadcasted_iota(jnp.int32, (256, 256), 0)
    i1 = lax.broadcasted_iota(jnp.int32, (256, 256), 1)
    upto = ((i1 <= i0) & (i1 // 32 == i0 // 32)).astype(F32).astype(BF16)
    rank = dot_t(needed.astype(BF16), upto) * needed
    rank_col = dot_t(upto, needed.astype(BF16))[:, 0:1]
    flags[0] = (rank > 2 * cap).astype(jnp.int32)
    y_copies = [
        go(remote(flags.at[0], flags.at[r], y_send.at[r], y_recv.at[r], {"grp": group(r)})) for r in (1, 2, 3)
    ]
    slot_block = lax.broadcasted_iota(jnp.int32, (256, 2 * lane), 1) // BLK + 1
    held = (rank_col == slot_block.astype(F32)).astype(F32).astype(BF16)
    chip = lax.broadcasted_iota(jnp.int32, (8, 256), 1) // 32 == lax.broadcasted_iota(jnp.int32, (8, 256), 0)
    numbers = jnp.where(chip, (table + 1).astype(F32) * needed, 0.0).astype(BF16)
    places = (dot(numbers, held).astype(jnp.int32) - 1) * BLK
    places_ref[...] = places + lax.rem(lax.broadcasted_iota(jnp.int32, (8, 2 * lane), 1), BLK)
    e0 = lax.broadcasted_iota(jnp.int32, (256, 1024), 0)
    e1 = lax.broadcasted_iota(jnp.int32, (256, 1024), 1)
    enlarge = (e1 // 32 + z * 32 == e0).astype(F32).astype(BF16)
    target = (dot(rank.astype(BF16), enlarge)[0:1].astype(jnp.int32) - 1) * (2 * BLK)
    target = target + lax.rem(lax.broadcasted_iota(jnp.int32, (1, 1024), 1), 2 * BLK)
    slot = lax.broadcasted_iota(jnp.int32, (2 * lane, 1024), 0)
    slot = jnp.where(slot >= lane, 2 * (slot - lane) + 1, 2 * slot) + core * (2 * lane)
    pick = (target == slot).astype(F32).astype(BF16)

    own_copy.wait()
    for c in x_copies:
        c.wait_recv()
    half = pl.ds(pl.multiple_of(core * 512, 512), 512)
    raw_side = go(remote(raw.at[half], raw.at[half], sib_send.at[0], sib_recv.at[0], {"tok": sib}))
    weights_start(0)
    arrive("s", 1)
    raw_side.wait_recv()
    packed = dot(pick, raw[...]).astype(BF16)
    pk[0, my_lane, 0:COLS] = packed[:lane]
    pk[0, my_lane, COLS : 2 * COLS] = packed[lane:]
    for part in range(parts):
        depart("m", 0, part)
        depart("p", 0, part)
    sides["p", 0] = go(pk_side(0))

    own_id = t * ROWS + lax.broadcasted_iota(jnp.int32, (ROWS, 256), 0)
    first = jnp.zeros((ROWS, 256), jnp.int32)
    end = jnp.int32(0)
    for i in range(8):
        length = lengths_ref[0, i]
        end = end + length
        first = first + jnp.where(own_id >= end, length, 0)
    low = jnp.maximum(first, own_id - (WINDOW - 1))
    beyond = NZ * 32 * BLK - WINDOW + own_id - first
    col = lax.broadcasted_iota(jnp.int32, (ROWS, 256), 1)

    def visible(kind, d):
        if kind == "s":
            ids = (z - d) * 256 + col
            return [(sfx, d, 0, (ids >= low) & (ids <= own_id))]
        d = d if kind == "p" else NZ - d
        row = lax.rem(z - d + NZ, NZ)
        out = []
        for j in range(2 * lane // 256):
            place = jnp.broadcast_to(places_ref[pl.ds(row, 1), j * 256 : (j + 1) * 256], (ROWS, 256))
            out.append((pk, d, j * 256, ((place >= 0) & (place < SINK)) | (place > beyond)))
        return out

    state = []

    def absorb(*chunks):
        views = []
        for kind, d in chunks:
            if d > hops[kind][1]:
                continue
            sides[kind, d].wait_recv()
            views += visible(kind, d)
        if not views:
            return
        top = state[0] if state else None
        scores = []
        for buf, d, start, allowed in views:
            s = dot_t(qbd[...], buf[d, start : start + 256, 0:COLS])
            s = jnp.where(allowed[None], s.reshape(4, ROWS, 256), MASKED).reshape(4 * ROWS, 256)
            scores.append(s)
        high = functools.reduce(jnp.maximum, [x[:, c : c + 128] for x in scores for c in (0, 128)])
        high = jnp.max(high, axis=-1, keepdims=True)
        if state:
            high = jnp.maximum(high, state[0])
            shrink = jnp.exp(state[0] - high)
            total, summed = state[1] * shrink, acc[...] * shrink
        else:
            total, summed = jnp.zeros((4 * ROWS, 128), F32), jnp.zeros((4 * ROWS, COLS), F32)
        for (buf, d, start, allowed), s in zip(views, scores):
            w = jnp.exp(s - high)
            total = total + w[:, 0:128] + w[:, 128:256]
            summed = summed + dot(w.astype(BF16), buf[d, start : start + 256, COLS : 2 * COLS])
        acc[...] = summed
        state[:] = [high, total]

    weights_start(1)
    for c in loads[7:]:
        c.start()
    absorb(("s", 0))
    weights_share(0)
    weights_start(2)
    absorb(("s", 1))
    absorb(("p", 0))
    arrive("s", 2)
    d0 = lax.broadcasted_iota(jnp.int32, (512, 512), 0)
    d1 = lax.broadcasted_iota(jnp.int32, (512, 512), 1)
    split = (jnp.where(d0 >= 256, 2 * d0 - 511, 2 * d0) == d1).astype(F32).astype(BF16)
    loads[3].wait()
    cross[h] = dot(split, cross_raw[...]).astype(BF16)
    arrive("m", 1)
    arrive("p", 1)
    weights_share(1)
    cross_start()
    absorb(("s", 2))
    absorb(("m", 1))
    arrive("s", 3)
    weights_share(2)
    absorb(("p", 1))
    arrive("m", 2)
    arrive("p", 2)
    absorb(("s", 3))
    absorb(("m", 2))
    arrive("s", 4)
    absorb(("p", 2))
    arrive("m", 3)
    arrive("p", 3)
    absorb(("s", 4))
    absorb(("m", 3))
    arrive("m", 4)
    absorb(("p", 3))
    absorb(("m", 4))
    attended = unstack_heads(acc[...], jnp.sum(state[1], axis=-1, keepdims=True), ROWS)

    my_share = pl.ds(pl.multiple_of(h * SHARE, SHARE), SHARE)

    def reduce_scatter(i, partial):
        rs_send[i] = partial.astype(BF16)
        copies = [
            go(
                remote(
                    rs_send.at[i, pl.ds(pl.multiple_of(peer(r) * SHARE, SHARE), SHARE)],
                    rs_recv.at[i, r],
                    rs_s.at[i, r],
                    rs_r.at[i, r],
                    {"head": peer(r)},
                )
            )
            for r in (2, 1, 3)
        ]
        total = rs_send[i, my_share, :].astype(F32)
        for c in copies:
            c.wait_recv()
        for r in (1, 2, 3):
            total = total + rs_recv[i, r].astype(F32)
        return total

    def all_gather(i, rows):
        ag[i, my_share, :] = rows
        copies = [
            go(
                remote(
                    ag.at[i, my_share], ag.at[i, my_share], ag_s.at[i, r], ag_r.at[i, r], {"head": peer(r)}
                )
            )
            for r in (2, 1, 3)
        ]
        for c in copies:
            c.wait_recv()
        return ag[i]

    at_send[...] = attended
    at_copies = [
        go(
            remote(
                at_send.at[pl.ds(pl.multiple_of(peer(r) * SHARE, SHARE), SHARE)],
                at_recv.at[h],
                at_s.at[r],
                at_r.at[r],
                {"head": peer(r)},
            )
        )
        for r in (2, 1, 3)
    ]
    at_recv[h] = at_send[my_share, :]
    weights_pass(0)
    cross_pass()
    weights_pass(1)
    weights_done(0)
    for c in at_copies:
        c.wait_recv()
    after_self = tokens_ref[my_share, :].astype(F32) + sum(dot(at_recv[i], wout[i]) for i in range(4))
    x = layer_norm(after_self).astype(BF16)
    weights_pass(2)
    weights_done(1)
    for r in (1, 3, 2):
        cross_z[r].wait_recv()
    outs = []
    for i in range(4):
        cq = (dot(x, wcq[i]) * (HEAD_DIM ** -0.5)).astype(BF16)
        s = dot_t(stack_heads(cq), cross[i, 0:256])
        w = jnp.exp(s - jnp.max(s, axis=-1, keepdims=True))
        outs.append(
            unstack_heads(dot(w.astype(BF16), cross[i, 256:512]), jnp.sum(w, axis=-1, keepdims=True), SHARE)
        )
    weights_done(2)
    after_cross = after_self + sum(dot(outs[i], wco[i]) for i in range(4))
    x = all_gather(0, layer_norm(after_cross).astype(BF16))
    loads[7].wait()
    hidden = jnp.maximum(dot(x, wup[...]), 0.0).astype(BF16)
    loads[8].wait()
    out_ref[...] = (after_cross + reduce_scatter(0, dot(hidden, wdown[...]))).astype(BF16)

    for c in y_copies:
        c.wait_recv()
    flag_ref[0, 0] = jnp.max(jnp.maximum(jnp.maximum(flags[0], flags[1]), jnp.maximum(flags[2], flags[3])))
    for c in sent:
        c.wait_send()


def run_layer(cap, plus_hops, parts, lengths, table, *arrays):
    lane = cap * BLK
    minus_hops = NZ - 1 - plus_hops
    dma = pltpu.SemaphoreType.DMA
    vmem = pl.BlockSpec(memory_space=pltpu.VMEM)
    smem = pl.BlockSpec(memory_space=pltpu.SMEM)
    return pl.pallas_call(
        functools.partial(layer_kernel, cap, plus_hops, parts),
        out_shape=(jax.ShapeDtypeStruct((SHARE, WIDTH), BF16), jax.ShapeDtypeStruct((1, 1), jnp.int32)),
        in_specs=[smem, vmem] + [pl.BlockSpec(memory_space=pltpu.HBM)] * len(arrays),
        out_specs=(vmem, smem),
        scratch_shapes=[
            pltpu.VMEM((ROWS, WIDTH), BF16),
            pltpu.VMEM((4, 512, COLS), BF16),
            pltpu.VMEM((WIDTH, COLS), BF16),
            pltpu.VMEM((2 * WIDTH, COLS), BF16),
            pltpu.VMEM((4, COLS, WIDTH), BF16),
            pltpu.VMEM((4, WIDTH, COLS), BF16),
            pltpu.VMEM((4, COLS, WIDTH), BF16),
            pltpu.VMEM((WIDTH, 2048), BF16),
            pltpu.VMEM((2048, WIDTH), BF16),
            pltpu.VMEM((128, WIDTH), BF16),
            pltpu.VMEM((1024, COLS), BF16),
            pltpu.VMEM((512, COLS), BF16),
            pltpu.VMEM((SFX_HOPS + 1, 256, 2 * COLS), BF16),
            pltpu.VMEM((NZ, 2 * lane, 2 * COLS), BF16),
            pltpu.VMEM((NZ, 2 * lane), jnp.int32),
            pltpu.VMEM((4 * ROWS, COLS), BF16),
            pltpu.VMEM((4 * ROWS, COLS), F32),
            pltpu.VMEM((ROWS, COLS), BF16),
            pltpu.VMEM((4, SHARE, COLS), BF16),
            pltpu.VMEM((1, ROWS, WIDTH), BF16),
            pltpu.VMEM((1, 4, SHARE, WIDTH), BF16),
            pltpu.VMEM((1, ROWS, WIDTH), BF16),
            pltpu.VMEM((4, 8, 256), jnp.int32),
            dma((9,)),
            dma((2,)),
            dma((4,)),
            dma((4,)),
            dma((4,)),
            dma((4,)),
            dma((1,)),
            dma((1,)),
            dma((SFX_HOPS + 1, parts)),
            dma((SFX_HOPS + 1, parts)),
            dma((SFX_HOPS + 1,)),
            dma((SFX_HOPS + 1,)),
            dma((plus_hops + 1, parts)),
            dma((plus_hops + 1, parts)),
            dma((minus_hops + 1, parts)),
            dma((minus_hops + 1, parts)),
            dma((NZ,)),
            dma((NZ,)),
            dma((4,)),
            dma((4,)),
            dma((1, 4)),
            dma((1, 4)),
            dma((1, 4)),
            dma((1, 4)),
            dma((3, 4)),
            dma((3, 4)),
            dma((3, 4, 4)),
            dma((3, 4, 4)),
            dma((3, 4)),
            dma((3, 4)),
            dma((4,)),
            dma((4,)),
            dma((4,)),
            dma((4,)),
        ],
        compiler_params=pltpu.CompilerParams(
            collective_id=cap // 16, has_side_effects=True, vmem_limit_bytes=63 << 20
        ),
    )(lengths, table, *arrays)


def on_device(
    tokens,
    lengths,
    block_position,
    prefix_pool,
    cross_cache,
    *weights,
):
    operands = (lengths, block_position, tokens[0], prefix_pool[0], cross_cache[0]) + weights
    out, overflow = run_layer(8, 3, 2, *operands)
    out = lax.cond(overflow[0, 0] > 0, lambda *_: run_layer(16, 3, 1, *operands)[0], lambda *_: out)
    return out[None]


def solution(mesh):
    return jax.shard_map(
        on_device,
        mesh=mesh,
        in_specs=(
            P("grp", "tok", None),
            P("grp", None),
            P("grp", None),
            P("grp", ("tok", "head"), None, None, None),
            P("grp", None, None, "head"),
            P(None, "head"),
            P(None, None, "head"),
            P("head", None),
            P(None, "head"),
            P("head", None),
            P(None, "head"),
            P("head", None),
        ),
        out_specs=P("grp", ("tok", "head"), None),
        check_vma=False,
    )
```

```python
import functools

import jax
import jax.numpy as jnp
from jax import lax
from jax.experimental import pallas as pl
from jax.experimental.pallas import tpu as pltpu
from jax.sharding import PartitionSpec as P

HEAD_DIM = 64
SINK = 4
WINDOW = 1024
EPS = 1e-05
MASKED = -1e30
MESH = pl.DeviceIdType.MESH

ROWS = 128
WIDTH = 1024
COLS = 256
SHARE = 32
BLK = 16
NZ = 8
SFX_HOPS = 4
F32 = jnp.float32
BF16 = jnp.bfloat16


def layer_norm(v):
    center = v - jnp.mean(v, axis=-1, keepdims=True)
    spread = jnp.mean(center * center, axis=-1, keepdims=True)
    return center * lax.rsqrt(spread + EPS)


def dot(a, b):
    return jnp.dot(a, b, preferred_element_type=F32)


def dot_t(a, b):
    return lax.dot_general(a, b, (((1,), (1,)), ((), ())), preferred_element_type=F32)


def stack_heads(q):
    head = lax.broadcasted_iota(jnp.int32, q.shape, 1) // HEAD_DIM
    zero = jnp.zeros_like(q)
    return jnp.concatenate([jnp.where(head == i, q, zero) for i in range(4)], axis=0)


def unstack_heads(summed, total, rows):
    head = lax.broadcasted_iota(jnp.int32, (rows, COLS), 1) // HEAD_DIM
    num = summed[0:rows]
    den = jnp.broadcast_to(total[0:rows], (rows, COLS))
    for i in range(1, 4):
        part = slice(i * rows, (i + 1) * rows)
        num = jnp.where(head == i, summed[part], num)
        den = jnp.where(head == i, jnp.broadcast_to(total[part], (rows, COLS)), den)
    return (num / den).astype(BF16)


def layer_kernel(
    cap,
    plus_hops,
    parts,
    lengths_ref,
    table_ref,
    tokens_hbm,
    pool_hbm,
    cross_hbm,
    wq_hbm,
    wkv_hbm,
    wout_hbm,
    wcq_hbm,
    wco_hbm,
    wup_hbm,
    wdown_hbm,
    out_ref,
    flag_ref,
    tokens_ref,
    cross,
    wq,
    wkv,
    wout,
    wcq,
    wco,
    wup,
    wdown,
    pool,
    raw,
    cross_raw,
    sfx,
    pk,
    places_ref,
    qbd,
    acc,
    at_send,
    at_recv,
    rs_send,
    rs_recv,
    ag,
    flags,
    w_sem,
    local_sem,
    x_send,
    x_recv,
    y_send,
    y_recv,
    sib_send,
    sib_recv,
    sfx_send,
    sfx_recv,
    sfx_sib_send,
    sfx_sib_recv,
    plus_send,
    plus_recv,
    minus_send,
    minus_recv,
    pk_sib_send,
    pk_sib_recv,
    at_s,
    at_r,
    rs_s,
    rs_r,
    ag_s,
    ag_r,
    wx_s,
    wx_r,
    wy_s,
    wy_r,
    wz_s,
    wz_r,
    cx_s,
    cx_r,
    cz_s,
    cz_r,
):
    minus_hops = NZ - 1 - plus_hops
    lane = cap * BLK
    g = lax.axis_index("grp")
    t = lax.axis_index("tok")
    h = lax.axis_index("head")
    core = lax.rem(t, 2)
    z = t // 2
    sib = t + 1 - 2 * core
    up = lax.rem(t + 2, 2 * NZ)
    down = lax.rem(t + 2 * NZ - 2, 2 * NZ)

    def peer(r):
        return lax.rem(h + r, 4)

    def group(r):
        return lax.rem(g + r, 4)

    loads = [
        pltpu.make_async_copy(src, dst, w_sem.at[i])
        for i, (src, dst) in enumerate(
            [
                (tokens_hbm, tokens_ref),
                (wkv_hbm.reshape(2 * WIDTH, COLS), wkv),
                (wq_hbm, wq),
                (cross_hbm.reshape(512, COLS), cross_raw),
                (wout_hbm, wout.at[h]),
                (wcq_hbm, wcq.at[h]),
                (wco_hbm, wco.at[h]),
                (wup_hbm, wup),
                (wdown_hbm, wdown),
            ]
        )
    ]
    pool_copy = pltpu.make_async_copy(pool_hbm.reshape(128, WIDTH), pool, local_sem.at[1])
    pool_copy.start()
    for c in loads[:3]:
        c.start()

    barrier = pltpu.get_barrier_semaphore()
    for dev in (
        [{"head": peer(r)} for r in (1, 2, 3)] + [{"grp": group(r)} for r in (1, 2, 3)] + [{"tok": i} for i in (sib, up, down)]
    ):
        pl.semaphore_signal(barrier, inc=1, device_id=dev, device_id_type=MESH)
    pl.semaphore_wait(barrier, 9)

    def remote(src, dst, send, recv, dev):
        return pltpu.make_async_remote_copy(
            src_ref=src, dst_ref=dst, send_sem=send, recv_sem=recv, device_id=dev, device_id_type=MESH
        )

    sent = []

    def go(c):
        c.start()
        sent.append(c)
        return c

    raw_rows = raw.at[pl.ds(pl.multiple_of(core * 512, 512) + pl.multiple_of(h * 128, 128), 128)]

    def pool_part(i):
        return pool.at[:, pl.ds(pl.multiple_of(i * COLS, COLS), COLS)]

    pool_copy.wait()
    x_copies = [
        go(remote(pool_part(peer(r)), raw_rows, x_send.at[r], x_recv.at[r], {"head": peer(r)})) for r in (2, 1, 3)
    ]
    own_copy = pltpu.make_async_copy(pool_part(h), raw_rows, local_sem.at[0])
    own_copy.start()
    for c in loads[3:7]:
        c.start()

    loads[0].wait()
    normed = layer_norm(tokens_ref[...].astype(F32)).astype(BF16)
    spread_row = lax.broadcasted_iota(jnp.int32, (128, 512), 0)
    spread_col = lax.broadcasted_iota(jnp.int32, (128, 512), 1)
    spread_to = 2 * spread_row + jnp.where(spread_col >= 256, 257, 0)
    spread = (spread_to == spread_col).astype(F32).astype(BF16)
    blocks = [normed[:, i * 128 : (i + 1) * 128] for i in range(8)]
    wide = dot(jnp.concatenate(blocks, axis=0), spread).astype(BF16)
    halves = [
        jnp.concatenate([wide[i * 128 : (i + 1) * 128, c : c + 256] for i in range(8)], axis=1) for c in (0, 256)
    ]
    my_rows = pl.ds(pl.multiple_of(core * ROWS, ROWS), ROWS)
    my_lane = pl.ds(pl.multiple_of(core * lane, lane), lane)
    loads[1].wait()
    kv = dot(jnp.concatenate(halves, axis=0), wkv[...]).astype(BF16)
    sfx[0, my_rows, 0:COLS] = kv[:ROWS]
    sfx[0, my_rows, COLS : 2 * COLS] = kv[ROWS:]

    def piece(start, rows, part):
        size = rows // parts
        return pl.ds(pl.multiple_of(start + part * size, size), size)

    def sfx_hop(d, part):
        rows = piece(core * ROWS, ROWS, part)
        return remote(
            sfx.at[d, rows], sfx.at[d + 1, rows], sfx_send.at[d + 1, part], sfx_recv.at[d + 1, part], {"tok": up}
        )

    def sfx_side(d):
        return remote(
            sfx.at[d, my_rows], sfx.at[d, my_rows], sfx_sib_send.at[d], sfx_sib_recv.at[d], {"tok": sib}
        )

    def plus_hop(d, part):
        rows = piece(core * lane, lane, part)
        return remote(
            pk.at[d, rows], pk.at[d + 1, rows], plus_send.at[d + 1, part], plus_recv.at[d + 1, part], {"tok": up}
        )

    def minus_hop(d, part):
        rows = piece(core * lane, lane, part)
        return remote(
            pk.at[(NZ - d) % NZ, rows],
            pk.at[NZ - d - 1, rows],
            minus_send.at[d + 1, part],
            minus_recv.at[d + 1, part],
            {"tok": down},
        )

    def pk_side(d):
        return remote(pk.at[d, my_lane], pk.at[d, my_lane], pk_sib_send.at[d], pk_sib_recv.at[d], {"tok": sib})

    hops = {"s": (sfx_hop, SFX_HOPS), "p": (plus_hop, plus_hops), "m": (minus_hop, minus_hops)}
    moving = {}
    sides = {}

    def depart(kind, d, part):
        moving[kind, d + 1, part] = go(hops[kind][0](d, part))

    def arrive(kind, d):
        if d > hops[kind][1]:
            return
        for part in range(parts):
            moving[kind, d, part].wait_recv()
            if d < hops[kind][1]:
                depart(kind, d, part)
        sides[kind, d] = go(sfx_side(d) if kind == "s" else pk_side(d if kind == "p" else NZ - d))

    for part in range(parts):
        depart("s", 0, part)
    sides["s", 0] = go(sfx_side(0))

    shared = [wout, wcq, wco]
    eighth = core * 4 + g

    def shard(r):
        return lax.rem(h + 4 - r, 4)

    def held_rows(i):
        size = shared[i].shape[1] // 8
        return pl.ds(pl.multiple_of(eighth * size, size), size)

    weights_x, weights_y, weights_z, cross_x, cross_z = {}, {}, {}, {}, {}

    def weights_start(i):
        loads[4 + i].wait()
        part = shared[i].at[h, held_rows(i)]
        for r in (1, 3, 2):
            weights_x[i, r] = go(remote(part, part, wx_s.at[i, r], wx_r.at[i, r], {"head": peer(r)}))

    def weights_share(i):
        for r in (1, 3, 2):
            weights_x[i, r].wait_recv()
            part = shared[i].at[shard(r), held_rows(i)]
            for q in (1, 3, 2):
                weights_y[i, r, q] = go(remote(part, part, wy_s.at[i, r, q], wy_r.at[i, r, q], {"grp": group(q)}))

    def weights_pass(i):
        size = shared[i].shape[1] // 2
        for r in (1, 3, 2):
            for q in (1, 3, 2):
                weights_y[i, r, q].wait_recv()
            part = shared[i].at[shard(r), pl.ds(pl.multiple_of(core * size, size), size)]
            weights_z[i, r] = go(remote(part, part, wz_s.at[i, r], wz_r.at[i, r], {"tok": sib}))

    def weights_done(i):
        for r in (1, 3, 2):
            weights_z[i, r].wait_recv()

    cross_rows = pl.ds(pl.multiple_of(core * 256, 256), 256)

    def cross_start():
        for r in (1, 3, 2):
            part = cross.at[h, cross_rows]
            cross_x[r] = go(remote(part, part, cx_s.at[r], cx_r.at[r], {"head": peer(r)}))

    def cross_pass():
        for r in (1, 3, 2):
            cross_x[r].wait_recv()
            part = cross.at[shard(r), cross_rows]
            cross_z[r] = go(remote(part, part, cz_s.at[r], cz_r.at[r], {"tok": sib}))

    loads[2].wait()
    q = (dot(normed, wq[...]) * (HEAD_DIM ** -0.5)).astype(BF16)
    qbd[...] = stack_heads(q)

    table = jnp.broadcast_to(table_ref[...], (8, 256))
    needed = ((table == 0) | (table >= 192)).astype(F32)
    i0 = lax.broadcasted_iota(jnp.int32, (256, 256), 0)
    i1 = lax.broadcasted_iota(jnp.int32, (256, 256), 1)
    upto = ((i1 <= i0) & (i1 // 32 == i0 // 32)).astype(F32).astype(BF16)
    rank = dot_t(needed.astype(BF16), upto) * needed
    rank_col = dot_t(upto, needed.astype(BF16))[:, 0:1]
    flags[0] = (rank > 2 * cap).astype(jnp.int32)
    y_copies = [
        go(remote(flags.at[0], flags.at[r], y_send.at[r], y_recv.at[r], {"grp": group(r)})) for r in (1, 2, 3)
    ]
    slot_block = lax.broadcasted_iota(jnp.int32, (256, 2 * lane), 1) // BLK + 1
    held = (rank_col == slot_block.astype(F32)).astype(F32).astype(BF16)
    chip = lax.broadcasted_iota(jnp.int32, (8, 256), 1) // 32 == lax.broadcasted_iota(jnp.int32, (8, 256), 0)
    numbers = jnp.where(chip, (table + 1).astype(F32) * needed, 0.0).astype(BF16)
    places = (dot(numbers, held).astype(jnp.int32) - 1) * BLK
    places_ref[...] = places + lax.rem(lax.broadcasted_iota(jnp.int32, (8, 2 * lane), 1), BLK)
    e0 = lax.broadcasted_iota(jnp.int32, (256, 1024), 0)
    e1 = lax.broadcasted_iota(jnp.int32, (256, 1024), 1)
    enlarge = (e1 // 32 + z * 32 == e0).astype(F32).astype(BF16)
    target = (dot(rank.astype(BF16), enlarge)[0:1].astype(jnp.int32) - 1) * (2 * BLK)
    target = target + lax.rem(lax.broadcasted_iota(jnp.int32, (1, 1024), 1), 2 * BLK)
    slot = lax.broadcasted_iota(jnp.int32, (2 * lane, 1024), 0)
    slot = jnp.where(slot >= lane, 2 * (slot - lane) + 1, 2 * slot) + core * (2 * lane)
    pick = (target == slot).astype(F32).astype(BF16)

    own_copy.wait()
    for c in x_copies:
        c.wait_recv()
    half = pl.ds(pl.multiple_of(core * 512, 512), 512)
    raw_side = go(remote(raw.at[half], raw.at[half], sib_send.at[0], sib_recv.at[0], {"tok": sib}))
    weights_start(0)
    arrive("s", 1)
    raw_side.wait_recv()
    packed = dot(pick, raw[...]).astype(BF16)
    pk[0, my_lane, 0:COLS] = packed[:lane]
    pk[0, my_lane, COLS : 2 * COLS] = packed[lane:]
    for part in range(parts):
        depart("m", 0, part)
        depart("p", 0, part)
    sides["p", 0] = go(pk_side(0))

    own_id = t * ROWS + lax.broadcasted_iota(jnp.int32, (ROWS, 256), 0)
    first = jnp.zeros((ROWS, 256), jnp.int32)
    end = jnp.int32(0)
    for i in range(8):
        length = lengths_ref[0, i]
        end = end + length
        first = first + jnp.where(own_id >= end, length, 0)
    low = jnp.maximum(first, own_id - (WINDOW - 1))
    beyond = NZ * 32 * BLK - WINDOW + own_id - first
    col = lax.broadcasted_iota(jnp.int32, (ROWS, 256), 1)

    def visible(kind, d):
        if kind == "s":
            ids = (z - d) * 256 + col
            return [(sfx, d, 0, (ids >= low) & (ids <= own_id))]
        d = d if kind == "p" else NZ - d
        row = lax.rem(z - d + NZ, NZ)
        out = []
        for j in range(2 * lane // 256):
            place = jnp.broadcast_to(places_ref[pl.ds(row, 1), j * 256 : (j + 1) * 256], (ROWS, 256))
            out.append((pk, d, j * 256, ((place >= 0) & (place < SINK)) | (place > beyond)))
        return out

    state = []

    def absorb(*chunks):
        views = []
        for kind, d in chunks:
            if d > hops[kind][1]:
                continue
            sides[kind, d].wait_recv()
            views += visible(kind, d)
        if not views:
            return
        top = state[0] if state else None
        scores = []
        for buf, d, start, allowed in views:
            s = dot_t(qbd[...], buf[d, start : start + 256, 0:COLS])
            s = jnp.where(allowed[None], s.reshape(4, ROWS, 256), MASKED).reshape(4 * ROWS, 256)
            scores.append(s)
        high = functools.reduce(jnp.maximum, [x[:, c : c + 128] for x in scores for c in (0, 128)])
        high = jnp.max(high, axis=-1, keepdims=True)
        if state:
            high = jnp.maximum(high, state[0])
            shrink = jnp.exp(state[0] - high)
            total, summed = state[1] * shrink, acc[...] * shrink
        else:
            total, summed = jnp.zeros((4 * ROWS, 128), F32), jnp.zeros((4 * ROWS, COLS), F32)
        for (buf, d, start, allowed), s in zip(views, scores):
            w = jnp.exp(s - high)
            total = total + w[:, 0:128] + w[:, 128:256]
            summed = summed + dot(w.astype(BF16), buf[d, start : start + 256, COLS : 2 * COLS])
        acc[...] = summed
        state[:] = [high, total]

    weights_start(1)
    for c in loads[7:]:
        c.start()
    absorb(("s", 0))
    weights_share(0)
    weights_start(2)
    absorb(("s", 1))
    absorb(("p", 0))
    arrive("s", 2)
    d0 = lax.broadcasted_iota(jnp.int32, (512, 512), 0)
    d1 = lax.broadcasted_iota(jnp.int32, (512, 512), 1)
    split = (jnp.where(d0 >= 256, 2 * d0 - 511, 2 * d0) == d1).astype(F32).astype(BF16)
    loads[3].wait()
    cross[h] = dot(split, cross_raw[...]).astype(BF16)
    arrive("m", 1)
    arrive("p", 1)
    weights_share(1)
    cross_start()
    absorb(("s", 2))
    absorb(("m", 1))
    arrive("s", 3)
    weights_share(2)
    absorb(("p", 1))
    arrive("m", 2)
    arrive("p", 2)
    absorb(("s", 3))
    absorb(("m", 2))
    arrive("s", 4)
    absorb(("p", 2))
    arrive("m", 3)
    arrive("p", 3)
    absorb(("s", 4))
    absorb(("m", 3))
    arrive("m", 4)
    absorb(("p", 3))
    absorb(("m", 4))
    attended = unstack_heads(acc[...], jnp.sum(state[1], axis=-1, keepdims=True), ROWS)

    my_share = pl.ds(pl.multiple_of(h * SHARE, SHARE), SHARE)

    def reduce_scatter(i, partial):
        rs_send[i] = partial.astype(BF16)
        copies = [
            go(
                remote(
                    rs_send.at[i, pl.ds(pl.multiple_of(peer(r) * SHARE, SHARE), SHARE)],
                    rs_recv.at[i, r],
                    rs_s.at[i, r],
                    rs_r.at[i, r],
                    {"head": peer(r)},
                )
            )
            for r in (2, 1, 3)
        ]
        total = rs_send[i, my_share, :].astype(F32)
        for c in copies:
            c.wait_recv()
        for r in (1, 2, 3):
            total = total + rs_recv[i, r].astype(F32)
        return total

    def all_gather(i, rows):
        ag[i, my_share, :] = rows
        copies = [
            go(
                remote(
                    ag.at[i, my_share], ag.at[i, my_share], ag_s.at[i, r], ag_r.at[i, r], {"head": peer(r)}
                )
            )
            for r in (2, 1, 3)
        ]
        for c in copies:
            c.wait_recv()
        return ag[i]

    at_send[...] = attended
    at_copies = [
        go(
            remote(
                at_send.at[pl.ds(pl.multiple_of(peer(r) * SHARE, SHARE), SHARE)],
                at_recv.at[h],
                at_s.at[r],
                at_r.at[r],
                {"head": peer(r)},
            )
        )
        for r in (2, 1, 3)
    ]
    at_recv[h] = at_send[my_share, :]
    weights_pass(0)
    cross_pass()
    weights_pass(1)
    weights_done(0)
    for c in at_copies:
        c.wait_recv()
    after_self = tokens_ref[my_share, :].astype(F32) + sum(dot(at_recv[i], wout[i]) for i in range(4))
    x = layer_norm(after_self).astype(BF16)
    weights_pass(2)
    weights_done(1)
    for r in (1, 3, 2):
        cross_z[r].wait_recv()
    outs = []
    for i in range(4):
        cq = (dot(x, wcq[i]) * (HEAD_DIM ** -0.5)).astype(BF16)
        s = dot_t(stack_heads(cq), cross[i, 0:256])
        w = jnp.exp(s - jnp.max(s, axis=-1, keepdims=True))
        outs.append(
            unstack_heads(dot(w.astype(BF16), cross[i, 256:512]), jnp.sum(w, axis=-1, keepdims=True), SHARE)
        )
    weights_done(2)
    after_cross = after_self + sum(dot(outs[i], wco[i]) for i in range(4))
    x = all_gather(0, layer_norm(after_cross).astype(BF16))
    loads[7].wait()
    hidden = jnp.maximum(dot(x, wup[...]), 0.0).astype(BF16)
    loads[8].wait()
    out_ref[...] = (after_cross + reduce_scatter(0, dot(hidden, wdown[...]))).astype(BF16)

    for c in y_copies:
        c.wait_recv()
    flag_ref[0, 0] = jnp.max(jnp.maximum(jnp.maximum(flags[0], flags[1]), jnp.maximum(flags[2], flags[3])))
    for c in sent:
        c.wait_send()


def run_layer(cap, plus_hops, parts, lengths, table, *arrays):
    lane = cap * BLK
    minus_hops = NZ - 1 - plus_hops
    dma = pltpu.SemaphoreType.DMA
    vmem = pl.BlockSpec(memory_space=pltpu.VMEM)
    smem = pl.BlockSpec(memory_space=pltpu.SMEM)
    return pl.pallas_call(
        functools.partial(layer_kernel, cap, plus_hops, parts),
        out_shape=(jax.ShapeDtypeStruct((SHARE, WIDTH), BF16), jax.ShapeDtypeStruct((1, 1), jnp.int32)),
        in_specs=[smem, vmem] + [pl.BlockSpec(memory_space=pltpu.HBM)] * len(arrays),
        out_specs=(vmem, smem),
        scratch_shapes=[
            pltpu.VMEM((ROWS, WIDTH), BF16),
            pltpu.VMEM((4, 512, COLS), BF16),
            pltpu.VMEM((WIDTH, COLS), BF16),
            pltpu.VMEM((2 * WIDTH, COLS), BF16),
            pltpu.VMEM((4, COLS, WIDTH), BF16),
            pltpu.VMEM((4, WIDTH, COLS), BF16),
            pltpu.VMEM((4, COLS, WIDTH), BF16),
            pltpu.VMEM((WIDTH, 2048), BF16),
            pltpu.VMEM((2048, WIDTH), BF16),
            pltpu.VMEM((128, WIDTH), BF16),
            pltpu.VMEM((1024, COLS), BF16),
            pltpu.VMEM((512, COLS), BF16),
            pltpu.VMEM((SFX_HOPS + 1, 256, 2 * COLS), BF16),
            pltpu.VMEM((NZ, 2 * lane, 2 * COLS), BF16),
            pltpu.VMEM((NZ, 2 * lane), jnp.int32),
            pltpu.VMEM((4 * ROWS, COLS), BF16),
            pltpu.VMEM((4 * ROWS, COLS), F32),
            pltpu.VMEM((ROWS, COLS), BF16),
            pltpu.VMEM((4, SHARE, COLS), BF16),
            pltpu.VMEM((1, ROWS, WIDTH), BF16),
            pltpu.VMEM((1, 4, SHARE, WIDTH), BF16),
            pltpu.VMEM((1, ROWS, WIDTH), BF16),
            pltpu.VMEM((4, 8, 256), jnp.int32),
            dma((9,)),
            dma((2,)),
            dma((4,)),
            dma((4,)),
            dma((4,)),
            dma((4,)),
            dma((1,)),
            dma((1,)),
            dma((SFX_HOPS + 1, parts)),
            dma((SFX_HOPS + 1, parts)),
            dma((SFX_HOPS + 1,)),
            dma((SFX_HOPS + 1,)),
            dma((plus_hops + 1, parts)),
            dma((plus_hops + 1, parts)),
            dma((minus_hops + 1, parts)),
            dma((minus_hops + 1, parts)),
            dma((NZ,)),
            dma((NZ,)),
            dma((4,)),
            dma((4,)),
            dma((1, 4)),
            dma((1, 4)),
            dma((1, 4)),
            dma((1, 4)),
            dma((3, 4)),
            dma((3, 4)),
            dma((3, 4, 4)),
            dma((3, 4, 4)),
            dma((3, 4)),
            dma((3, 4)),
            dma((4,)),
            dma((4,)),
            dma((4,)),
            dma((4,)),
        ],
        compiler_params=pltpu.CompilerParams(
            collective_id=cap // 16, has_side_effects=True, vmem_limit_bytes=63 << 20
        ),
    )(lengths, table, *arrays)


def on_device(
    tokens,
    lengths,
    block_position,
    prefix_pool,
    cross_cache,
    *weights,
):
    operands = (lengths, block_position, tokens[0], prefix_pool[0], cross_cache[0]) + weights
    out, overflow = run_layer(8, 3, 1, *operands)
    out = lax.cond(overflow[0, 0] > 0, lambda *_: run_layer(16, 3, 1, *operands)[0], lambda *_: out)
    return out[None]


def solution(mesh):
    return jax.shard_map(
        on_device,
        mesh=mesh,
        in_specs=(
            P("grp", "tok", None),
            P("grp", None),
            P("grp", None),
            P("grp", ("tok", "head"), None, None, None),
            P("grp", None, None, "head"),
            P(None, "head"),
            P(None, None, "head"),
            P("head", None),
            P(None, "head"),
            P("head", None),
            P(None, "head"),
            P("head", None),
        ),
        out_specs=P("grp", ("tok", "head"), None),
        check_vma=False,
    )
```
